32 devices in a mesh: dom: 8 (over z, core), cls: 4 (over y, x).
Axes of the slice: x: 2, y: 2, z: 4, core: 2. Of those that a mesh axis runs over, the one named last changes fastest.
Arguments:
- particles: bfloat16 [768, 2048], P('dom', 'cls'), may hold values from -12 to 12
- references: float32 [32, 36, 2048], P('cls', None, 'dom'), may hold values from -0.4 to 0.4
- noise_weight: float32 [1024], replicated, may hold values from 0.5 to 2
Outputs:
- class_sums: float32 [32, 36, 2048], P('cls', None, 'dom')
- class_weight: float32 [32, 36], P('cls')
The draws below stay inside these ranges and needn't reach their ends.
All inputs are finite; a program needn't handle non-finite values.
Results may differ from the reference program's by a relative error of at most 0.0033.
Values may be sent and summed in bfloat16 or wider, within the bound.
No kernel may reach another device: no remote copies, remote signals or barrier semaphores. Data moves between devices by JAX's collectives and lax.ppermute only.
A program may use at most 64 MiB of HBM per device.

```python
import math
import jax
import jax.numpy as jnp
from jax import lax

WIN = 32
BOX = 64
F = 2048
K = 32
R = 36
SHIFT_SIDE = 9
P_SIZE = 768


def base_references(key):
    values = jax.random.normal(jax.random.fold_in(key, 11), (K, R, F), jnp.float32) * (1.92 / WIN)
    return jnp.clip(values, -0.4, 0.4)


def draw_references(key, part):
    return base_references(key)


def draw_particles(key, part):
    noise = jax.random.normal(jax.random.fold_in(key, 12), (P_SIZE, F), jnp.float32)
    noise = jnp.clip(noise, -5.0, 5.0)
    table = base_references(key).reshape(K * R, F)
    picks = jax.random.randint(jax.random.fold_in(key, 14), (8,), 0, K * R)
    chosen = jnp.arange(8) * (P_SIZE // 8)
    strength = (12.0 + 4.0 * jnp.arange(8)).astype(jnp.float32)[:, None]
    aligned = strength * table[picks] + (strength - 0.25) * table[(picks + R) % (K * R)] + 0.3 * noise[chosen]
    noise = noise.at[chosen].set(aligned)
    return jnp.clip(noise, -12.0, 12.0).astype(jnp.bfloat16)


def setup_inputs(seed: int = 0) -> dict:
    seeds = jax.random.split(jax.random.key(seed), 4)
    particles = draw_particles(jax.random.fold_in(seeds[3], 71), 0)
    references = draw_references(jax.random.fold_in(seeds[3], 71), 0)
    noise_weight = jnp.clip(jnp.exp(jax.random.uniform(seeds[2], (WIN * WIN,), jnp.float32, math.log(0.5), math.log(2.0))), 0.5, 2.0)
    return dict(particles=particles, references=references, noise_weight=noise_weight)


def phase_tables():
    freq = jnp.arange(WIN * WIN)
    freq_y = (freq // WIN - WIN // 2).astype(jnp.float32)
    freq_x = (freq % WIN - WIN // 2).astype(jnp.float32)
    offset = jnp.arange(SHIFT_SIDE * SHIFT_SIDE)
    shift_y = (offset // SHIFT_SIDE - SHIFT_SIDE // 2).astype(jnp.float32)
    shift_x = (offset % SHIFT_SIDE - SHIFT_SIDE // 2).astype(jnp.float32)
    theta = (2.0 * math.pi / BOX) * (shift_x[:, None] * freq_x[None, :] + shift_y[:, None] * freq_y[None, :])
    return jnp.cos(theta), jnp.sin(theta)


def shifted_block(real_part, imag_part, cosine, sine):
    moved_real = real_part[None] * cosine[:, None] + imag_part[None] * sine[:, None]
    moved_imag = imag_part[None] * cosine[:, None] - real_part[None] * sine[:, None]
    return jnp.concatenate([moved_real, moved_imag], axis=2).astype(jnp.bfloat16)


def reference(particles, references, noise_weight):
    quarter = WIN * WIN
    real_part = particles[:, :quarter].astype(jnp.float32)
    imag_part = particles[:, quarter:].astype(jnp.float32)
    weight_full = jnp.concatenate([noise_weight, noise_weight])
    weighted = (references * weight_full).astype(jnp.bfloat16).reshape(K * R, F)
    half_flat = (0.5 * jnp.sum(references * references * weight_full, axis=2)).reshape(K * R)
    cosine, sine = phase_tables()

    def scores_at(cos_row, sin_row):
        moved = shifted_block(real_part, imag_part, cos_row[None], sin_row[None])[0]
        return moved, jnp.dot(moved, weighted.T, preferred_element_type=jnp.float32) - half_flat

    def first_pass(carry, rows):
        peak, total = carry
        _, scores = scores_at(rows[0], rows[1])
        new_peak = jnp.maximum(peak, jnp.max(scores, axis=1))
        total = total * jnp.exp(peak - new_peak) + jnp.sum(jnp.exp(scores - new_peak[:, None]), axis=1)
        return (new_peak, total), None

    start = (jnp.full((P_SIZE,), -jnp.inf, jnp.float32), jnp.zeros((P_SIZE,), jnp.float32))
    (peak, total), _ = lax.scan(first_pass, start, (cosine, sine))

    def second_pass(carry, rows):
        sums, weights_total = carry
        moved, scores = scores_at(rows[0], rows[1])
        probs = jnp.exp(scores - peak[:, None]) / total[:, None]
        probs_low = probs.astype(jnp.bfloat16)
        sums = sums + jnp.dot(probs_low.T, moved, preferred_element_type=jnp.float32)
        weights_total = weights_total + jnp.sum(probs, axis=0)
        return (sums, weights_total), None

    start_two = (jnp.zeros((K * R, F), jnp.float32), jnp.zeros((K * R,), jnp.float32))
    (sums, weights_total), _ = lax.scan(second_pass, start_two, (cosine, sine))
    return sums.reshape(K, R, F), weights_total.reshape(K, R)
```

```python
import math

import jax
import jax.numpy as jnp
import numpy as np
from jax import lax
from jax.experimental import pallas as pl
from jax.experimental.pallas import tpu as pltpu
from jax.sharding import PartitionSpec as P

WIN = 32
BOX = 64
SHIFT_SIDE = 9
SHIFTS = SHIFT_SIDE * SHIFT_SIDE
HALF = WIN * WIN
F = 2 * HALF
GROUP = 8
MAIN = SHIFTS // GROUP * GROUP
STEPS = MAIN // GROUP
TAIL = 16
F32 = jnp.float32
BF16 = jnp.bfloat16
PARAMS = pltpu.CompilerParams(vmem_limit_bytes=48 * 1024 * 1024)


def phase_tables():
    freq = np.arange(HALF)
    fy = freq // WIN - WIN // 2
    fx = freq % WIN - WIN // 2
    offset = np.arange(SHIFTS)
    sy = offset // SHIFT_SIDE - SHIFT_SIDE // 2
    sx = offset % SHIFT_SIDE - SHIFT_SIDE // 2
    turns = sx[:, None] * fx[None, :] + sy[:, None] * fy[None, :]
    theta = (2.0 * math.pi / BOX) * turns
    pad = -SHIFTS % GROUP
    cosine = np.pad(np.cos(theta), ((0, pad), (0, 0))).astype(np.float32)
    sine = np.pad(np.sin(theta), ((0, pad), (0, 0))).astype(np.float32)
    return cosine, sine


def contract(x, y, dims):
    return lax.dot_general(x, y, (dims, ((), ())), preferred_element_type=F32)


def spread(row):
    high = row.astype(BF16).astype(F32)
    rest = row - high
    mid = rest.astype(BF16).astype(F32)
    low = (rest - mid).astype(BF16).astype(F32)
    return high, mid, low


def column_to_row(column, length, scratch):
    h = column.shape[0]
    scratch[...] = jnp.zeros(scratch.shape, F32)
    scratch[0:h, :] = jnp.broadcast_to(column, (h, 128))
    return scratch[...].T[0:1, :]


def tail_block(row, width, scratch):
    scratch[...] = jnp.zeros(scratch.shape, F32)
    per = row.shape[1] // width
    for p, part in enumerate(spread(row)):
        for j in range(per):
            r = p * per + j
            scratch[r : r + 1, :] = part[:, j * width : (j + 1) * width]
    return scratch[...].astype(BF16)


def row_of_tail(tail, width, length):
    per = length // width
    pieces = []
    for j in range(per):
        rows = [tail[p * per + j : p * per + j + 1, :] for p in range(3)]
        pieces.append((rows[2] + rows[1]) + rows[0])
    return jnp.concatenate(pieces, axis=1) if per > 1 else pieces[0]


def prepare_body(where, refs, noise, message, flat, tall, tail):
    classes, rotations, width = refs.shape
    h = classes * rotations
    for k in range(classes):
        flat[k * rotations : (k + 1) * rotations, :] = refs[k]
    x = flat[...]
    w = noise[...]
    message[0:h, :] = (x * w).astype(BF16)
    half = 0.5 * jnp.sum(x * x * w, axis=1, keepdims=True)
    row = column_to_row(half, tall.shape[0], tall)
    message[h : h + TAIL, :] = tail_block(row, width, tail)


def shift_body(where, *refs, parts, width):
    pieces = refs[:parts]
    cosine, sine, rest_cos, rest_sin, out, rest, whole = refs[parts:]
    rows = whole.shape[0]

    @pl.when(pl.program_id(0) == 0)
    def _():
        for k in range(parts):
            at = pl.multiple_of(jnp.bitwise_xor(where[2], k) * width, 128)
            whole[:, pl.ds(at, width)] = pieces[k][...].astype(F32)

    def move(c, s, target, at):
        for q in range(0, HALF, 256):
            a = whole[:, q : q + 256]
            b = whole[:, HALF + q : HALF + q + 256]
            cq = c[:, q : q + 256]
            sq = s[:, q : q + 256]
            target[at : at + rows, q : q + 256] = (a * cq + b * sq).astype(BF16)
            target[at : at + rows, HALF + q : HALF + q + 256] = (b * cq - a * sq).astype(BF16)

    for j in range(GROUP):
        move(cosine[j : j + 1, :], sine[j : j + 1, :], out, j * rows)

    @pl.when(pl.program_id(0) == 0)
    def _():
        move(rest_cos[0:1, :], rest_sin[0:1, :], rest, 0)


def score_body(where, *refs, parts, width, length):
    pieces = refs[:parts]
    moved, moved_rest, scores, scores_rest, stats, weighted, half, top, total = refs[parts:]
    h = weighted.shape[0]
    rows = moved_rest.shape[0]
    step = pl.program_id(0)

    @pl.when(step == 0)
    def _():
        row = jnp.zeros((1, length), F32)
        for k in range(parts):
            at = pl.multiple_of(jnp.bitwise_xor(where[0], k) * width, 128)
            weighted[:, pl.ds(at, width)] = pieces[k][0:h, :]
            row += row_of_tail(pieces[k][h : h + TAIL, :].astype(F32), width, length)
        half[...] = jnp.broadcast_to(row, (128, length)).T[0:h, :]
        top[...] = jnp.full(top.shape, -jnp.inf, F32)
        total[...] = jnp.zeros(total.shape, F32)

    block = contract(weighted[...], moved[...], ((1,), (1,))) - half[:, 0:1]
    scores[...] = block
    old = top[...]
    new = jnp.maximum(old, jnp.max(block, axis=0, keepdims=True))
    total[...] = total[...] * jnp.exp(old - new) + jnp.sum(
        jnp.exp(block - new), axis=0, keepdims=True
    )
    top[...] = new

    @pl.when(step == pl.num_programs(0) - 1)
    def _():
        last = contract(weighted[...], moved_rest[...], ((1,), (1,))) - half[:, 0:1]
        scores_rest[...] = last
        tops = [top[:, j * rows : (j + 1) * rows] for j in range(GROUP)]
        best = jnp.max(last, axis=0, keepdims=True)
        for t in tops:
            best = jnp.maximum(best, t)
        mass = jnp.sum(jnp.exp(last - best), axis=0, keepdims=True)
        for j in range(GROUP):
            mass += total[:, j * rows : (j + 1) * rows] * jnp.exp(tops[j] - best)
        stats[...] = jnp.zeros(stats.shape, F32)
        stats[0:1, 0:rows] = best
        stats[1:2, 0:rows] = mass


def first_sums_body(where, *refs, groups, length):
    gathered = refs[:groups]
    (scores, scores_rest, moved, moved_rest, probs, probs_rest, own, other, weight_row) = refs[
        groups : groups + 9
    ]
    sums, top, inverse, mass, tall, tail = refs[groups + 9 :]
    h, width = own.shape
    rows = moved_rest.shape[0]
    step = pl.program_id(0)

    @pl.when(step == 0)
    def _():
        best = gathered[0][0:1, 0:rows]
        for g in gathered[1:]:
            best = jnp.maximum(best, g[0:1, 0:rows])
        whole = jnp.zeros((1, rows), F32)
        for g in gathered:
            whole += g[1:2, 0:rows] * jnp.exp(g[0:1, 0:rows] - best)
        scale = 1.0 / whole
        for j in range(GROUP):
            top[:, j * rows : (j + 1) * rows] = best
            inverse[:, j * rows : (j + 1) * rows] = scale
        last = jnp.exp(scores_rest[...] - best) * scale
        last_low = last.astype(BF16)
        probs_rest[...] = last_low
        mass[...] = jnp.zeros(mass.shape, F32)
        mass[:, 0:1] = jnp.sum(last, axis=1, keepdims=True)
        sums[...] = contract(last_low, moved_rest[...], ((1,), (0,)))

    prob = jnp.exp(scores[...] - top[...]) * inverse[...]
    low = prob.astype(BF16)
    probs[...] = low
    part = prob[:, 0:128]
    for j in range(128, GROUP * rows, 128):
        part += prob[:, j : j + 128]
    mass[...] += part
    sums[...] += contract(low, moved[...], ((1,), (0,)))

    @pl.when(step == pl.num_programs(0) - 1)
    def _():
        here = pl.multiple_of(where[1] * width, 128)
        there = pl.multiple_of((1 - where[1]) * width, 128)
        own[...] = sums[:, pl.ds(here, width)]
        other[0:h, :] = sums[:, pl.ds(there, width)].astype(BF16)
        row = column_to_row(jnp.sum(mass[...], axis=1, keepdims=True), length, tall)
        weight_row[...] = jnp.broadcast_to(row, weight_row.shape)
        other[h : h + TAIL, :] = tail_block(row, width, tail)


def sums_body(where, probs, probs_rest, moved, moved_rest, own, other, sums):
    width = own.shape[1]
    step = pl.program_id(0)

    @pl.when(step == 0)
    def _():
        sums[...] = contract(probs_rest[...], moved_rest[...], ((1,), (0,)))

    sums[...] += contract(probs[...], moved[...], ((1,), (0,)))

    @pl.when(step == pl.num_programs(0) - 1)
    def _():
        here = pl.multiple_of(where[1] * width, 128)
        there = pl.multiple_of((1 - where[1]) * width, 128)
        own[...] = sums[:, pl.ds(here, width)]
        other[...] = sums[:, pl.ds(there, width)].astype(BF16)


def first_pair_body(own, received, weight_row, message, chip_row, tail):
    h, width = own.shape
    message[0:h, :] = (own[...] + received[0:h, :].astype(F32)).astype(BF16)
    length = weight_row.shape[1]
    row = weight_row[0:1, :] + row_of_tail(received[h : h + TAIL, :].astype(F32), width, length)
    chip_row[...] = jnp.broadcast_to(row, chip_row.shape)
    message[h : h + TAIL, :] = tail_block(row, width, tail)


def pair_body(own, received, first, message):
    h = own.shape[0]
    message[0:h, :] = (own[...] + received[...].astype(F32)).astype(BF16)
    message[h : h + TAIL, :] = first[h : h + TAIL, :]


def finish_body(*refs, count):
    messages = refs[:count]
    own, received, chip_row, class_sums, class_weight, flat = refs[count:]
    h, width = own.shape
    classes, rotations, _ = class_sums.shape
    length = chip_row.shape[1]
    x = own[...] + received[...].astype(F32)
    row = chip_row[0:1, :]
    for m in messages:
        x += m[0:h, :].astype(F32)
        row += row_of_tail(m[h : h + TAIL, :].astype(F32), width, length)
    flat[...] = x
    for k in range(classes):
        class_sums[k] = flat[k * rotations : (k + 1) * rotations, :]
        class_weight[k : k + 1, :] = row[:, k * rotations : (k + 1) * rotations]


def full(shape):
    return pl.BlockSpec(shape, lambda *_: (0,) * len(shape))


def make_on_device(dom, cls):
    pairs = dom // 2

    def swap(x, axis, size, k):
        return lax.ppermute(x, axis, [(i, i ^ k) for i in range(size)])

    def on_device(particles, references, noise_weight):
        rows, part_width = particles.shape
        classes, rotations, width = references.shape
        h = classes * rotations
        length = -(-h // width) * width
        block = GROUP * rows
        shape = jax.ShapeDtypeStruct
        place = lax.axis_index("dom")
        column = lax.axis_index("cls")
        where = jnp.stack([place, place % 2, column]).astype(jnp.int32)

        def call(body, grid, ins, outs, shapes, scratch, name, scalars=True):
            spec = pltpu.PrefetchScalarGridSpec(
                num_scalar_prefetch=1 if scalars else 0,
                grid=grid,
                in_specs=ins,
                out_specs=outs,
                scratch_shapes=scratch,
            )
            return pl.pallas_call(
                body, grid_spec=spec, out_shape=shapes, compiler_params=PARAMS, name=name
            )

        pieces = [particles] + [swap(particles, "cls", cls, k) for k in range(1, cls)]

        slabs = HALF // width
        message = call(
            prepare_body,
            (1,),
            [
                full((classes, rotations, width)),
                pl.BlockSpec((1, width), lambda i, w: (0, w[0] % slabs)),
            ],
            full((h + TAIL, width)),
            shape((h + TAIL, width), BF16),
            [
                pltpu.VMEM((h, width), F32),
                pltpu.VMEM((length, 128), F32),
                pltpu.VMEM((TAIL, width), F32),
            ],
            "prepare",
        )(where, references, noise_weight.reshape(1, HALF))

        even = [message] + [swap(message, "dom", dom, 2 * k) for k in range(1, pairs)]
        odd = [swap(m, "dom", dom, 1) for m in even]
        slices = [m for both in zip(even, odd) for m in both]

        cosine, sine = phase_tables()
        moved, moved_rest = call(
            lambda *r: shift_body(*r, parts=cls, width=part_width),
            (STEPS,),
            [full((rows, part_width))] * cls
            + [pl.BlockSpec((GROUP, HALF), lambda i, w: (i, 0))] * 2
            + [pl.BlockSpec((GROUP, HALF), lambda i, w: (STEPS, 0))] * 2,
            [pl.BlockSpec((block, F), lambda i, w: (i, 0)), full((rows, F))],
            [shape((MAIN * rows, F), BF16), shape((rows, F), BF16)],
            [pltpu.VMEM((rows, F), F32)],
            "shift",
        )(where, *pieces, cosine, sine, cosine, sine)

        scores, scores_rest, stats = call(
            lambda *r: score_body(*r, parts=dom, width=width, length=length),
            (STEPS,),
            [full((h + TAIL, width))] * dom
            + [pl.BlockSpec((block, F), lambda i, w: (i, 0)), full((rows, F))],
            [
                pl.BlockSpec((h, block), lambda i, w: (0, i)),
                full((h, rows)),
                full((8, 128)),
            ],
            [
                shape((h, MAIN * rows), F32),
                shape((h, rows), F32),
                shape((8, 128), F32),
            ],
            [
                pltpu.VMEM((h, F), BF16),
                pltpu.VMEM((h, 128), F32),
                pltpu.VMEM((1, block), F32),
                pltpu.VMEM((1, block), F32),
            ],
            "score",
        )(where, *slices, moved, moved_rest)

        gathered = [stats] + [swap(stats, "cls", cls, k) for k in range(1, cls)]

        def moved_specs(k):
            def at(w):
                return jnp.bitwise_xor(w[0] // 2, k)

            return [
                pl.BlockSpec((block, 2 * width), lambda i, w: (i, at(w))),
                pl.BlockSpec((rows, 2 * width), lambda i, w: (0, at(w))),
            ]

        prob_specs = [pl.BlockSpec((h, block), lambda i, w: (0, i)), full((h, rows))]
        accumulator = pltpu.VMEM((h, 2 * width), F32)
        order = list(range(pairs - 1, -1, -1))
        messages = []
        probs, probs_rest, own, other, weight_row = call(
            lambda *r: first_sums_body(*r, groups=cls, length=length),
            (STEPS,),
            [full((8, 128))] * cls + prob_specs + moved_specs(order[0]),
            prob_specs + [full((h, width)), full((h + TAIL, width)), full((8, length))],
            [
                shape((h, MAIN * rows), BF16),
                shape((h, rows), BF16),
                shape((h, width), F32),
                shape((h + TAIL, width), BF16),
                shape((8, length), F32),
            ],
            [
                accumulator,
                pltpu.VMEM((1, block), F32),
                pltpu.VMEM((1, block), F32),
                pltpu.VMEM((h, 128), F32),
                pltpu.VMEM((length, 128), F32),
                pltpu.VMEM((TAIL, width), F32),
            ],
            "sums_first",
        )(where, *gathered, scores, scores_rest, moved, moved_rest)
        received = swap(other, "dom", dom, 1)
        first, chip_row = call(
            first_pair_body,
            (1,),
            [full((h, width)), full((h + TAIL, width)), full((8, length))],
            [full((h + TAIL, width)), full((8, length))],
            [shape((h + TAIL, width), BF16), shape((8, length), F32)],
            [pltpu.VMEM((TAIL, width), F32)],
            "pair_first",
            scalars=False,
        )(own, received, weight_row)
        messages.append(swap(first, "dom", dom, 2 * order[0]))

        for k in order[1:]:
            own, other = call(
                sums_body,
                (STEPS,),
                prob_specs + moved_specs(k),
                [full((h, width)), full((h, width))],
                [shape((h, width), F32), shape((h, width), BF16)],
                [accumulator],
                "sums",
            )(where, probs, probs_rest, moved, moved_rest)
            received = swap(other, "dom", dom, 1)
            if k:
                summed = call(
                    pair_body,
                    (1,),
                    [full((h, width)), full((h, width)), full((h + TAIL, width))],
                    full((h + TAIL, width)),
                    shape((h + TAIL, width), BF16),
                    [],
                    "pair",
                    scalars=False,
                )(own, received, first)
                messages.append(swap(summed, "dom", dom, 2 * k))

        return call(
            lambda *r: finish_body(*r, count=len(messages)),
            (1,),
            [full((h + TAIL, width))] * len(messages)
            + [full((h, width)), full((h, width)), full((8, length))],
            [full((classes, rotations, width)), full((classes, rotations))],
            [
                shape((classes, rotations, width), F32),
                shape((classes, rotations), F32),
            ],
            [pltpu.VMEM((h, width), F32)],
            "finish",
            scalars=False,
        )(*messages, own, received, chip_row)

    return on_device


def solution(mesh):
    return jax.shard_map(
        make_on_device(mesh.shape["dom"], mesh.shape["cls"]),
        mesh=mesh,
        in_specs=(P("dom", "cls"), P("cls", None, "dom"), P()),
        out_specs=(P("cls", None, "dom"), P("cls", None)),
        check_vma=False,
    )
```

```python
import math

import jax
import jax.numpy as jnp
import numpy as np
from jax import lax
from jax.experimental import pallas as pl
from jax.experimental.pallas import tpu as pltpu
from jax.sharding import PartitionSpec as P

WIN = 32
BOX = 64
SHIFT_SIDE = 9
SHIFTS = SHIFT_SIDE * SHIFT_SIDE
HALF = WIN * WIN
F = 2 * HALF
GROUP = 8
MAIN = SHIFTS // GROUP * GROUP
STEPS = MAIN // GROUP
TAIL = 16
F32 = jnp.float32
BF16 = jnp.bfloat16


def phase_tables():
    freq = np.arange(HALF)
    fy = freq // WIN - WIN // 2
    fx = freq % WIN - WIN // 2
    offset = np.arange(SHIFTS)
    sy = offset // SHIFT_SIDE - SHIFT_SIDE // 2
    sx = offset % SHIFT_SIDE - SHIFT_SIDE // 2
    turns = sx[:, None] * fx[None, :] + sy[:, None] * fy[None, :]
    theta = (2.0 * math.pi / BOX) * turns
    pad = -SHIFTS % GROUP
    cosine = np.pad(np.cos(theta), ((0, pad), (0, 0))).astype(np.float32)
    sine = np.pad(np.sin(theta), ((0, pad), (0, 0))).astype(np.float32)
    return cosine, sine


def contract(x, y, dims):
    return lax.dot_general(x, y, (dims, ((), ())), preferred_element_type=F32)


def spread(row):
    high = row.astype(BF16).astype(F32)
    rest = row - high
    mid = rest.astype(BF16).astype(F32)
    low = (rest - mid).astype(BF16).astype(F32)
    return high, mid, low


def column_to_row(column, length, scratch):
    h = column.shape[0]
    scratch[...] = jnp.zeros(scratch.shape, F32)
    scratch[0:h, :] = jnp.broadcast_to(column, (h, 128))
    return scratch[...].T[0:1, :]


def tail_block(row, width, scratch):
    scratch[...] = jnp.zeros(scratch.shape, F32)
    per = row.shape[1] // width
    for p, part in enumerate(spread(row)):
        for j in range(per):
            r = p * per + j
            scratch[r : r + 1, :] = part[:, j * width : (j + 1) * width]
    return scratch[...].astype(BF16)


def row_of_tail(tail, width, length):
    per = length // width
    pieces = []
    for j in range(per):
        rows = [tail[p * per + j : p * per + j + 1, :] for p in range(3)]
        pieces.append((rows[2] + rows[1]) + rows[0])
    return jnp.concatenate(pieces, axis=1) if per > 1 else pieces[0]


def prepare_body(where, refs, noise, message, tall, tail):
    h, width = refs.shape
    x = refs[...]
    w = noise[...]
    message[0:h, :] = (x * w).astype(BF16)
    half = 0.5 * jnp.sum(x * x * w, axis=1, keepdims=True)
    row = column_to_row(half, tall.shape[0], tall)
    message[h : h + TAIL, :] = tail_block(row, width, tail)


def table_body(where, tables, cosine, sine, *, width):
    count = HALF // width
    sign = jnp.where(where[0] < count, 1.0, -1.0).astype(F32)
    for k in range(count):
        at = pl.multiple_of(jnp.bitwise_and(jnp.bitwise_xor(where[0], k), count - 1) * width, 128)
        cosine[:, k * width : (k + 1) * width] = tables[0, :, pl.ds(at, width)]
        sine[:, k * width : (k + 1) * width] = tables[1, :, pl.ds(at, width)] * sign


def shift_body(where, *refs, parts, pairs, width):
    pieces = refs[:parts]
    cosine, sine = refs[parts : parts + 2]
    outs = refs[parts + 2 : parts + 2 + pairs]
    rest, plain, whole = refs[parts + 2 + pairs :]
    rows, part_width = pieces[0].shape
    for k in range(parts):
        at = pl.multiple_of(jnp.bitwise_xor(where[2], k) * part_width, 128)
        plain[:, pl.ds(at, part_width)] = pieces[k][...].astype(F32)
    for k in range(2 * pairs):
        at = pl.multiple_of(jnp.bitwise_xor(where[0], k) * width, 128)
        whole[:, k * width : (k + 1) * width] = plain[:, pl.ds(at, width)]

    def move(s, store):
        c_all = cosine[pl.ds(s, 1), :]
        s_all = sine[pl.ds(s, 1), :]
        for k in range(pairs):
            q = k * width
            c_row = c_all[:, q : q + width]
            s_row = s_all[:, q : q + width]
            a = whole[:, q : q + width]
            b = whole[:, HALF + q : HALF + q + width]
            store(k, (a * c_row + b * s_row).astype(BF16))
            store(k + pairs, (b * c_row - a * s_row).astype(BF16))

    def one(s, carry):
        at = pl.multiple_of(s * rows, rows)

        def store(k, value):
            outs[k // 2][pl.ds(at, rows), (k % 2) * width : (k % 2 + 1) * width] = value

        move(s, store)
        return carry

    lax.fori_loop(0, MAIN, one, 0)

    def store_rest(k, value):
        rest[:, k * width : (k + 1) * width] = value

    for s in range(MAIN, SHIFTS):
        move(s, store_rest)


def score_body(*refs, parts, pairs, length):
    pieces = refs[:parts]
    moved = refs[parts : parts + pairs]
    moved_rest = refs[parts + pairs]
    weights, weights_rest, tops, stats = refs[parts + pairs + 1 : parts + pairs + 5]
    weighted, half, even, odd, totals = refs[-5:]
    h, block = even.shape
    rows = moved_rest.shape[0]
    width = pieces[0].shape[1]

    row = jnp.zeros((1, length), F32)
    for k in range(parts):
        weighted[:, k * width : (k + 1) * width] = pieces[k][0:h, :]
        row += row_of_tail(pieces[k][h : h + TAIL, :].astype(F32), width, length)
    half[...] = jnp.broadcast_to(row, (128, length)).T[0:h, :]

    def multiply(i, target):
        at = i * block if isinstance(i, int) else pl.multiple_of(i * block, block)
        x = jnp.concatenate([m[pl.ds(at, block), :] for m in moved], axis=1)
        target[...] = contract(weighted[...], x, ((1,), (1,)))

    def soften(i, source):
        for q in range(0, block, 128):
            x = source[:, q : q + 128] - half[...]
            top = jnp.max(x, axis=0, keepdims=True)
            x = jnp.exp(x - top)
            weights[i, :, q : q + 128] = x
            tops[i, :, q : q + 128] = jnp.broadcast_to(top, (8, 128))
            total = jnp.sum(x, axis=0, keepdims=True)
            totals[i, :, q : q + 128] = jnp.broadcast_to(total, (8, 128))

    multiply(0, even)

    def two(t, carry):
        multiply(2 * t + 1, odd)
        soften(2 * t, even)
        multiply(2 * t + 2, even)
        soften(2 * t + 1, odd)
        return carry

    lax.fori_loop(0, STEPS // 2 - 1, two, 0)
    multiply(STEPS - 1, odd)
    soften(STEPS - 2, even)
    last = contract(weighted[...], moved_rest[...], ((1,), (1,))) - half[:, 0:1]
    soften(STEPS - 1, odd)

    best = jnp.max(last, axis=0, keepdims=True)
    last = jnp.exp(last - best)
    weights_rest[...] = last
    tops[STEPS, 0:1, 0:rows] = best
    mass = jnp.sum(last, axis=0, keepdims=True)
    lane_top = tops[0]
    for i in range(1, STEPS):
        lane_top = jnp.maximum(lane_top, tops[i])
    lane_mass = totals[0] * jnp.exp(tops[0] - lane_top)
    for i in range(1, STEPS):
        lane_mass += totals[i] * jnp.exp(tops[i] - lane_top)
    parts_top = [lane_top[0:1, j * rows : (j + 1) * rows] for j in range(GROUP)]
    peak = best
    for t in parts_top:
        peak = jnp.maximum(peak, t)
    mass = mass * jnp.exp(best - peak)
    for j in range(GROUP):
        mass += lane_mass[0:1, j * rows : (j + 1) * rows] * jnp.exp(parts_top[j] - peak)
    stats[...] = jnp.zeros(stats.shape, F32)
    stats[0:1, 0:rows] = peak
    stats[1:2, 0:rows] = mass


def split_pair(sums, own, other):
    h, width = own.shape
    own[...] = sums[:, 0:width]
    other[0:h, :] = sums[:, width : 2 * width].astype(BF16)


def accumulate(sums, probs, probs_rest, moved, moved_rest, rest_at):
    block = probs.shape[2]
    sums[...] = contract(probs_rest[...], moved_rest[:, rest_at : rest_at + sums.shape[1]], ((1,), (0,)))
    for i in range(STEPS):
        sums[...] += contract(probs[i], moved[i * block : (i + 1) * block, :], ((1,), (0,)))


def first_sums_body(*refs, groups, others, length, rest_at):
    gathered = refs[:groups]
    weights, weights_rest, tops, moved, moved_rest = refs[groups : groups + 5]
    probs, probs_rest, own, other, weight_row = refs[groups + 5 + others : groups + 10 + others]
    sums, peak, inverse, scale, mass, tall, tail = refs[-7:]
    h, width = own.shape
    rows = moved_rest.shape[0]
    block = probs.shape[2]

    best = gathered[0][0:1, 0:rows]
    for g in gathered[1:]:
        best = jnp.maximum(best, g[0:1, 0:rows])
    whole = jnp.zeros((1, rows), F32)
    for g in gathered:
        whole += g[1:2, 0:rows] * jnp.exp(g[0:1, 0:rows] - best)
    over = 1.0 / whole
    for j in range(GROUP):
        peak[:, j * rows : (j + 1) * rows] = jnp.broadcast_to(best, (8, rows))
        inverse[:, j * rows : (j + 1) * rows] = jnp.broadcast_to(over, (8, rows))
    for i in range(STEPS):
        scale[i] = jnp.exp(tops[i] - peak[...]) * inverse[...]

    last = weights_rest[...] * (jnp.exp(tops[STEPS, 0:1, 0:rows] - best) * over)
    last_low = last.astype(BF16)
    probs_rest[...] = last_low
    mass[...] = jnp.zeros(mass.shape, F32)
    mass[:, 0:1] = jnp.sum(last, axis=1, keepdims=True)
    for i in range(STEPS):
        part = mass[...]
        for q in range(0, block, 128):
            prob = weights[i, :, q : q + 128] * scale[i, 0:1, q : q + 128]
            probs[i, :, q : q + 128] = prob.astype(BF16)
            part += prob
        mass[...] = part
    accumulate(sums, probs, probs_rest, moved, moved_rest, rest_at)
    split_pair(sums, own, other)
    row = column_to_row(jnp.sum(mass[...], axis=1, keepdims=True), length, tall)
    weight_row[...] = jnp.broadcast_to(row, weight_row.shape)
    other[h : h + TAIL, :] = tail_block(row, width, tail)


def sums_body(probs, probs_rest, moved, moved_rest, *refs, others, rest_at):
    own, other = refs[others : others + 2]
    sums = refs[-1]
    accumulate(sums, probs, probs_rest, moved, moved_rest, rest_at)
    split_pair(sums, own, other)


def first_pair_body(own, received, weight_row, message, chip_row, tail):
    h, width = own.shape
    message[0:h, :] = (own[...] + received[0:h, :].astype(F32)).astype(BF16)
    length = weight_row.shape[1]
    row = weight_row[0:1, :] + row_of_tail(received[h : h + TAIL, :].astype(F32), width, length)
    chip_row[...] = jnp.broadcast_to(row, chip_row.shape)
    message[h : h + TAIL, :] = tail_block(row, width, tail)


def pair_body(own, received, first, message):
    h = own.shape[0]
    message[0:h, :] = (own[...] + received[...].astype(F32)).astype(BF16)
    message[h : h + TAIL, :] = first[h : h + TAIL, :]


def finish_body(*refs, count):
    messages = refs[:count]
    own, received, chip_row, class_sums, class_weight = refs[count:]
    h, width = own.shape
    rotations, classes = class_weight.shape[1], class_weight.shape[0]
    length = chip_row.shape[1]
    x = own[...] + received[...].astype(F32)
    row = chip_row[0:1, :]
    for m in messages:
        x += m[0:h, :].astype(F32)
        row += row_of_tail(m[h : h + TAIL, :].astype(F32), width, length)
    class_sums[...] = x
    shape = (classes, length)
    at = lax.broadcasted_iota(jnp.int32, shape, 1)
    mine = at - at // classes * classes == lax.broadcasted_iota(jnp.int32, shape, 0)
    spread_out = jnp.where(mine, jnp.broadcast_to(row, shape), 0.0)
    shape = (length, rotations)
    pick = lax.broadcasted_iota(jnp.int32, shape, 0) // classes == lax.broadcasted_iota(
        jnp.int32, shape, 1
    )
    class_weight[...] = lax.dot_general(
        spread_out,
        pick.astype(F32),
        (((1,), (0,)), ((), ())),
        precision=lax.Precision.HIGHEST,
        preferred_element_type=F32,
    )


VMEM = pl.BlockSpec(memory_space=pltpu.VMEM)


def make_on_device(dom, cls):
    pairs = dom // 2

    def swap(x, axis, size, k):
        return lax.ppermute(x, axis, [(i, i ^ k) for i in range(size)])

    def on_device(particles, references, noise_weight):
        rows, part_width = particles.shape
        classes, rotations, width = references.shape
        h = classes * rotations
        length = -(-h // width) * width
        block = GROUP * rows
        shape = jax.ShapeDtypeStruct
        place = lax.axis_index("dom")
        where = jnp.stack([place, place % 2, lax.axis_index("cls")]).astype(jnp.int32)

        def call(body, shapes, name, scratch=(), limit=2, aliases=None):
            def run(*args):
                scalars = args[0] is where
                specs = [VMEM] * (len(args) - scalars)
                spec = pltpu.PrefetchScalarGridSpec(
                    num_scalar_prefetch=int(scalars),
                    grid=(),
                    in_specs=specs,
                    out_specs=[VMEM] * len(shapes),
                    scratch_shapes=list(scratch),
                )
                params = pltpu.CompilerParams(vmem_limit_bytes=limit * 1024 * 1024)
                return pl.pallas_call(
                    body,
                    grid_spec=spec,
                    out_shape=shapes,
                    compiler_params=params,
                    input_output_aliases=aliases or {},
                    name=name,
                )(*args)

            return run

        pieces = [particles] + [swap(particles, "cls", cls, k) for k in range(1, cls)]

        ref_rows = references.transpose(1, 0, 2).reshape(h, width)
        slab = lax.dynamic_slice_in_dim(noise_weight, (place % pairs) * width, width)
        (message,) = call(
            lambda *r: prepare_body(None, *r),
            [shape((h + TAIL, width), BF16)],
            "prepare",
            [pltpu.VMEM((length, 128), F32), pltpu.VMEM((TAIL, width), F32)],
        )(ref_rows, slab.reshape(1, width))

        even = [message] + [swap(message, "dom", dom, 2 * k) for k in range(1, pairs)]
        odd = [swap(m, "dom", dom, 1) for m in even]
        slices = [m for both in zip(even, odd) for m in both]

        tables = np.stack(phase_tables())
        angles = call(
            lambda *r: table_body(*r, width=width),
            [shape(tables.shape[1:], F32)] * 2,
            "tables",
        )(where, tables)

        *moved, moved_rest = call(
            lambda *r: shift_body(*r, parts=cls, pairs=pairs, width=width),
            [pltpu.VMEM((MAIN * rows, 2 * width), BF16)] * pairs + [shape((rows, F), BF16)],
            "shift",
            limit=4,
            scratch=[pltpu.VMEM((rows, F), F32)] * 2,
        )(where, *pieces, *angles)

        weights, weights_rest, tops, stats, *moved = call(
            lambda *r: score_body(*r, parts=dom, pairs=pairs, length=length),
            [
                shape((STEPS, h, block), F32),
                shape((h, rows), F32),
                shape((STEPS + 1, 8, block), F32),
                shape((8, 128), F32),
            ]
            + [pltpu.VMEM((MAIN * rows, 2 * width), BF16)] * pairs,
            "score",
            aliases={dom + k: 4 + k for k in range(pairs)},
            limit=7,
            scratch=[
                pltpu.VMEM((h, F), BF16),
                pltpu.VMEM((h, 128), F32),
                pltpu.VMEM((h, block), F32),
                pltpu.VMEM((h, block), F32),
                pltpu.VMEM((STEPS, 8, block), F32),
            ],
        )(*slices, *moved, moved_rest)

        gathered = [stats] + [swap(stats, "cls", cls, k) for k in range(1, cls)]

        accumulator = pltpu.VMEM((h, 2 * width), F32)
        order = list(range(pairs - 1, -1, -1))
        messages = []
        probs, probs_rest, own, other, weight_row, *kept = call(
            lambda *r: first_sums_body(
                *r, groups=cls, others=pairs - 1, length=length, rest_at=order[0] * 2 * width
            ),
            [
                shape((STEPS, h, block), BF16),
                shape((h, rows), BF16),
                shape((h, width), F32),
                shape((h + TAIL, width), BF16),
                shape((8, length), F32),
            ]
            + [pltpu.VMEM((MAIN * rows, 2 * width), BF16)] * (pairs - 1),
            "sums_first",
            aliases={cls + 5 + k: 5 + k for k in range(pairs - 1)},
            limit=4,
            scratch=[
                accumulator,
                pltpu.VMEM((8, block), F32),
                pltpu.VMEM((8, block), F32),
                pltpu.VMEM(tops.shape, F32),
                pltpu.VMEM((h, 128), F32),
                pltpu.VMEM((length, 128), F32),
                pltpu.VMEM((TAIL, width), F32),
            ],
        )(*gathered, weights, weights_rest, tops, moved[order[0]], moved_rest, *moved[:-1])
        received = swap(other, "dom", dom, 1)
        first, chip_row = call(
            first_pair_body,
            [shape((h + TAIL, width), BF16), shape((8, length), F32)],
            "pair_first",
            [pltpu.VMEM((TAIL, width), F32)],
        )(own, received, weight_row)
        messages.append(swap(first, "dom", dom, 2 * order[0]))

        for k in order[1:]:
            own, other, *kept = call(
                lambda *r: sums_body(*r, others=k, rest_at=k * 2 * width),
                [shape((h, width), F32), shape((h, width), BF16)]
                + [pltpu.VMEM((MAIN * rows, 2 * width), BF16)] * k,
                "sums",
                [accumulator],
                aliases={4 + j: 2 + j for j in range(k)},
            )(probs, probs_rest, kept[k], moved_rest, *kept[:k])
            received = swap(other, "dom", dom, 1)
            if k:
                (summed,) = call(pair_body, [shape((h + TAIL, width), BF16)], "pair")(
                    own, received, first
                )
                messages.append(swap(summed, "dom", dom, 2 * k))

        sums, class_weight = call(
            lambda *r: finish_body(*r, count=len(messages)),
            [shape((h, width), F32), shape((classes, rotations), F32)],
            "finish",
        )(*messages, own, received, chip_row)
        return sums.reshape(rotations, classes, width).transpose(1, 0, 2), class_weight

    return on_device


def solution(mesh):
    return jax.shard_map(
        make_on_device(mesh.shape["dom"], mesh.shape["cls"]),
        mesh=mesh,
        in_specs=(P("dom", "cls"), P("cls", None, "dom"), P()),
        out_specs=(P("cls", None, "dom"), P("cls", None)),
        check_vma=False,
    )
```

```python
import math

import jax
import jax.numpy as jnp
import numpy as np
from jax import lax
from jax.experimental import pallas as pl
from jax.experimental.pallas import tpu as pltpu
from jax.sharding import PartitionSpec as P

WIN = 32
BOX = 64
SHIFT_SIDE = 9
SHIFTS = SHIFT_SIDE * SHIFT_SIDE
HALF = WIN * WIN
F = 2 * HALF
GROUP = 8
MAIN = SHIFTS // GROUP * GROUP
STEPS = MAIN // GROUP
TAIL = 16
F32 = jnp.float32
BF16 = jnp.bfloat16


def phase_tables():
    freq = np.arange(HALF)
    fy = freq // WIN - WIN // 2
    fx = freq % WIN - WIN // 2
    offset = np.arange(MAIN // 2)
    sy = offset // SHIFT_SIDE - SHIFT_SIDE // 2
    sx = offset % SHIFT_SIDE - SHIFT_SIDE // 2
    turns = sx[:, None] * fx[None, :] + sy[:, None] * fy[None, :]
    theta = (2.0 * math.pi / BOX) * turns
    return np.stack([np.cos(theta), np.sin(theta)]).astype(np.float32)


def contract(x, y, dims):
    return lax.dot_general(x, y, (dims, ((), ())), preferred_element_type=F32)


def spread(row):
    high = row.astype(BF16).astype(F32)
    rest = row - high
    mid = rest.astype(BF16).astype(F32)
    low = (rest - mid).astype(BF16).astype(F32)
    return high, mid, low


def column_to_row(column, length, scratch):
    h = column.shape[0]
    scratch[...] = jnp.zeros(scratch.shape, F32)
    scratch[0:h, :] = jnp.broadcast_to(column, (h, 128))
    return scratch[...].T[0:1, :]


def tail_block(row, width, scratch):
    scratch[...] = jnp.zeros(scratch.shape, F32)
    per = row.shape[1] // width
    for p, part in enumerate(spread(row)):
        for j in range(per):
            r = p * per + j
            scratch[r : r + 1, :] = part[:, j * width : (j + 1) * width]
    return scratch[...].astype(BF16)


def row_of_tail(tail, width, length):
    per = length // width
    pieces = []
    for j in range(per):
        rows = [tail[p * per + j : p * per + j + 1, :] for p in range(3)]
        pieces.append((rows[2] + rows[1]) + rows[0])
    return jnp.concatenate(pieces, axis=1) if per > 1 else pieces[0]


def prepare_body(where, refs, noise, message, tall, tail):
    h, width = refs.shape
    at = pl.multiple_of(jnp.bitwise_and(where[0], HALF // width - 1) * width, 128)
    x = refs[...]
    w = noise[:, pl.ds(at, width)]
    message[0:h, :] = (x * w).astype(BF16)
    half = 0.5 * jnp.sum(x * x * w, axis=1, keepdims=True)
    row = column_to_row(half, tall.shape[0], tall)
    message[h : h + TAIL, :] = tail_block(row, width, tail)


def table_body(where, tables, particles, cosine, sine, kept, *, width):
    kept[...] = particles[...]
    count = HALF // width
    sign = jnp.where(where[0] < count, 1.0, -1.0).astype(F32)
    for k in range(count):
        at = pl.multiple_of(jnp.bitwise_and(jnp.bitwise_xor(where[0], k), count - 1) * width, 128)
        cosine[:, k * width : (k + 1) * width] = tables[0, :, pl.ds(at, width)]
        sine[:, k * width : (k + 1) * width] = tables[1, :, pl.ds(at, width)] * sign


def shift_body(where, *refs, parts, pairs, width):
    pieces = refs[:parts]
    cosine, sine = refs[parts : parts + 2]
    outs = refs[parts + 2 : parts + 2 + pairs]
    rest, plain, whole = refs[parts + 2 + pairs :]
    rows, part_width = pieces[0].shape
    for k in range(parts):
        at = pl.multiple_of(jnp.bitwise_xor(where[2], k) * part_width, 128)
        plain[:, pl.ds(at, part_width)] = pieces[k][...].astype(F32)
    for k in range(2 * pairs):
        at = pl.multiple_of(jnp.bitwise_xor(where[0], k) * width, 128)
        whole[:, k * width : (k + 1) * width] = plain[:, pl.ds(at, width)]
    rest[...] = whole[...].astype(BF16)

    def one(s, carry):
        at = pl.multiple_of(2 * s * rows, rows)
        back = pl.multiple_of((2 * s + 1) * rows, rows)
        c_all = cosine[pl.ds(s, 1), :]
        s_all = sine[pl.ds(s, 1), :]
        for k in range(pairs):
            q = k * width
            c_row = c_all[:, q : q + width]
            s_row = s_all[:, q : q + width]
            a = whole[:, q : q + width]
            b = whole[:, HALF + q : HALF + q + width]
            ac, bs, bc, sa = a * c_row, b * s_row, b * c_row, a * s_row
            low = slice((k % 2) * width, (k % 2 + 1) * width)
            outs[k // 2][pl.ds(at, rows), low] = (ac + bs).astype(BF16)
            outs[(k + pairs) // 2][pl.ds(at, rows), low] = (bc - sa).astype(BF16)
            outs[k // 2][pl.ds(back, rows), low] = (ac - bs).astype(BF16)
            outs[(k + pairs) // 2][pl.ds(back, rows), low] = (bc + sa).astype(BF16)
        return carry

    lax.fori_loop(0, MAIN // 2, one, 0)


def stage_body(*refs, first, others, length, rest_at):
    mine, sibling, moved, moved_rest = refs[:4]
    count = 4 if first else 7
    partial = None if first else refs[4:7]
    scores, scores_rest, norms = refs[count + others : count + others + 3]
    weighted = refs[-1]
    h, span = weighted.shape
    width = span // 2
    block = scores.shape[2]
    row = jnp.zeros((1, length), F32) if first else partial[2][0:1, :]
    for k, piece in enumerate((mine, sibling)):
        weighted[:, k * width : (k + 1) * width] = piece[0:h, :]
        row += row_of_tail(piece[h : h + TAIL, :].astype(F32), width, length)
    norms[...] = jnp.broadcast_to(row, norms.shape)
    last = contract(weighted[...], moved_rest[:, rest_at : rest_at + span], ((1,), (1,)))
    scores_rest[...] = last if first else partial[1][...] + last
    for i in range(STEPS):
        x = contract(weighted[...], moved[i * block : (i + 1) * block, :], ((1,), (1,)))
        scores[i] = x if first else partial[0][i] + x


def last_stage_body(*refs, others, length, rest_at):
    mine, sibling, moved, moved_rest, scores, scores_rest, norms = refs[:7]
    weights, weights_rest, tops, stats = refs[7 + others : 11 + others]
    weighted, half, even, odd, totals = refs[-5:]
    h, block = even.shape
    rows = moved_rest.shape[0]
    span = weighted.shape[1]
    width = span // 2
    row = norms[0:1, :]
    for k, piece in enumerate((mine, sibling)):
        weighted[:, k * width : (k + 1) * width] = piece[0:h, :]
        row += row_of_tail(piece[h : h + TAIL, :].astype(F32), width, length)
    half[...] = jnp.broadcast_to(row, (128, length)).T[0:h, :]

    def multiply(i, target):
        x = contract(weighted[...], moved[i * block : (i + 1) * block, :], ((1,), (1,)))
        target[...] = scores[i] + x

    def soften(i, source):
        for q in range(0, block, 128):
            x = source[:, q : q + 128] - half[...]
            top = jnp.max(x, axis=0, keepdims=True)
            x = jnp.exp(x - top)
            weights[i, :, q : q + 128] = x
            tops[i, :, q : q + 128] = jnp.broadcast_to(top, (8, 128))
            total = jnp.sum(x, axis=0, keepdims=True)
            totals[i, :, q : q + 128] = jnp.broadcast_to(total, (8, 128))

    multiply(0, even)
    for i in range(1, STEPS):
        multiply(i, odd if i % 2 else even)
        soften(i - 1, even if i % 2 else odd)
    last = contract(weighted[...], moved_rest[:, rest_at : rest_at + span], ((1,), (1,)))
    last = scores_rest[...] + last - half[:, 0:1]
    soften(STEPS - 1, odd if (STEPS - 1) % 2 else even)

    best = jnp.max(last, axis=0, keepdims=True)
    last = jnp.exp(last - best)
    weights_rest[...] = last
    tops[STEPS, 0:1, 0:rows] = best
    mass = jnp.sum(last, axis=0, keepdims=True)
    lane_top = tops[0]
    for i in range(1, STEPS):
        lane_top = jnp.maximum(lane_top, tops[i])
    lane_mass = totals[0] * jnp.exp(tops[0] - lane_top)
    for i in range(1, STEPS):
        lane_mass += totals[i] * jnp.exp(tops[i] - lane_top)
    parts_top = [lane_top[0:1, j * rows : (j + 1) * rows] for j in range(GROUP)]
    peak = best
    for t in parts_top:
        peak = jnp.maximum(peak, t)
    mass = mass * jnp.exp(best - peak)
    for j in range(GROUP):
        mass += lane_mass[0:1, j * rows : (j + 1) * rows] * jnp.exp(parts_top[j] - peak)
    stats[...] = jnp.zeros(stats.shape, F32)
    stats[0:1, 0:rows] = peak
    stats[1:2, 0:rows] = mass


def split_pair(sums, own, other):
    h, width = own.shape
    own[...] = sums[:, 0:width]
    other[0:h, :] = sums[:, width : 2 * width].astype(BF16)


def accumulate(sums, probs, probs_rest, moved, moved_rest, rest_at, ahead=None):
    block = probs.shape[2]
    if ahead:
        ahead(0)
    sums[...] = contract(probs_rest[...], moved_rest[:, rest_at : rest_at + sums.shape[1]], ((1,), (0,)))
    for i in range(STEPS):
        if ahead and i + 1 < STEPS:
            ahead(i + 1)
        sums[...] += contract(probs[i], moved[i * block : (i + 1) * block, :], ((1,), (0,)))


def first_sums_body(*refs, groups, others, length, rest_at):
    gathered = refs[:groups]
    weights, weights_rest, tops, moved, moved_rest = refs[groups : groups + 5]
    probs, probs_rest, own, other, weight_row = refs[groups + 5 + others : groups + 10 + others]
    sums, peak, inverse, scale, mass, tall, tail = refs[-7:]
    h, width = own.shape
    rows = moved_rest.shape[0]
    block = probs.shape[2]

    best = gathered[0][0:1, 0:rows]
    for g in gathered[1:]:
        best = jnp.maximum(best, g[0:1, 0:rows])
    whole = jnp.zeros((1, rows), F32)
    for g in gathered:
        whole += g[1:2, 0:rows] * jnp.exp(g[0:1, 0:rows] - best)
    over = 1.0 / whole
    for j in range(GROUP):
        peak[:, j * rows : (j + 1) * rows] = jnp.broadcast_to(best, (8, rows))
        inverse[:, j * rows : (j + 1) * rows] = jnp.broadcast_to(over, (8, rows))
    for i in range(STEPS):
        scale[i] = jnp.exp(tops[i] - peak[...]) * inverse[...]

    last = weights_rest[...] * (jnp.exp(tops[STEPS, 0:1, 0:rows] - best) * over)
    last_low = last.astype(BF16)
    probs_rest[...] = last_low
    mass[...] = jnp.zeros(mass.shape, F32)
    mass[:, 0:1] = jnp.sum(last, axis=1, keepdims=True)

    def normalise(i):
        part = mass[...]
        for q in range(0, block, 128):
            prob = weights[i, :, q : q + 128] * scale[i, 0:1, q : q + 128]
            probs[i, :, q : q + 128] = prob.astype(BF16)
            part += prob
        mass[...] = part

    accumulate(sums, probs, probs_rest, moved, moved_rest, rest_at, normalise)
    split_pair(sums, own, other)
    row = column_to_row(jnp.sum(mass[...], axis=1, keepdims=True), length, tall)
    weight_row[...] = jnp.broadcast_to(row, weight_row.shape)
    other[h : h + TAIL, :] = tail_block(row, width, tail)


def sums_body(probs, probs_rest, moved, moved_rest, *refs, others, rest_at):
    own, other = refs[others : others + 2]
    sums = refs[-1]
    accumulate(sums, probs, probs_rest, moved, moved_rest, rest_at)
    split_pair(sums, own, other)


def first_pair_body(own, received, weight_row, message, chip_row, tail):
    h, width = own.shape
    message[0:h, :] = (own[...] + received[0:h, :].astype(F32)).astype(BF16)
    length = weight_row.shape[1]
    row = weight_row[0:1, :] + row_of_tail(received[h : h + TAIL, :].astype(F32), width, length)
    chip_row[...] = jnp.broadcast_to(row, chip_row.shape)
    message[h : h + TAIL, :] = tail_block(row, width, tail)


def pair_body(own, received, first, message):
    h = own.shape[0]
    message[0:h, :] = (own[...] + received[...].astype(F32)).astype(BF16)
    message[h : h + TAIL, :] = first[h : h + TAIL, :]


def finish_body(*refs, count):
    messages = refs[:count]
    own, received, chip_row, class_sums, class_weight = refs[count:]
    h, width = own.shape
    rotations, classes = class_weight.shape[1], class_weight.shape[0]
    length = chip_row.shape[1]
    x = own[...] + received[...].astype(F32)
    row = chip_row[0:1, :]
    for m in messages:
        x += m[0:h, :].astype(F32)
        row += row_of_tail(m[h : h + TAIL, :].astype(F32), width, length)
    class_sums[...] = x
    shape = (classes, length)
    at = lax.broadcasted_iota(jnp.int32, shape, 1)
    mine = at - at // classes * classes == lax.broadcasted_iota(jnp.int32, shape, 0)
    spread_out = jnp.where(mine, jnp.broadcast_to(row, shape), 0.0)
    shape = (length, rotations)
    pick = lax.broadcasted_iota(jnp.int32, shape, 0) // classes == lax.broadcasted_iota(
        jnp.int32, shape, 1
    )
    class_weight[...] = lax.dot_general(
        spread_out,
        pick.astype(F32),
        (((1,), (0,)), ((), ())),
        precision=lax.Precision.HIGHEST,
        preferred_element_type=F32,
    )


VMEM = pl.BlockSpec(memory_space=pltpu.VMEM)


def make_on_device(dom, cls):
    pairs = dom // 2

    def swap(x, axis, size, k):
        return lax.ppermute(x, axis, [(i, i ^ k) for i in range(size)])

    def on_device(particles, references, noise_weight):
        rows, part_width = particles.shape
        classes, rotations, width = references.shape
        h = classes * rotations
        length = -(-h // width) * width
        block = GROUP * rows
        shape = jax.ShapeDtypeStruct
        place = lax.axis_index("dom")
        where = jnp.stack([place, place % 2, lax.axis_index("cls")]).astype(jnp.int32)

        def call(body, shapes, name, scratch=(), limit=2, aliases=None):
            def run(*args):
                scalars = args[0] is where
                specs = [VMEM] * (len(args) - scalars)
                spec = pltpu.PrefetchScalarGridSpec(
                    num_scalar_prefetch=int(scalars),
                    grid=(),
                    in_specs=specs,
                    out_specs=[VMEM] * len(shapes),
                    scratch_shapes=list(scratch),
                )
                params = pltpu.CompilerParams(vmem_limit_bytes=limit * 1024 * 1024)
                return pl.pallas_call(
                    body,
                    grid_spec=spec,
                    out_shape=shapes,
                    compiler_params=params,
                    input_output_aliases=aliases or {},
                    cost_estimate=pl.CostEstimate(flops=1, transcendentals=0, bytes_accessed=1),
                    name=name,
                )(*args)

            return run

        pieces = [particles] + [swap(particles, "cls", cls, k) for k in range(1, cls)]

        ref_rows = references.transpose(1, 0, 2).reshape(h, width)
        (message,) = call(
            prepare_body,
            [shape((h + TAIL, width), BF16)],
            "prepare",
            [pltpu.VMEM((length, 128), F32), pltpu.VMEM((TAIL, width), F32)],
        )(where, ref_rows, noise_weight.reshape(1, HALF))

        even = [message] + [swap(message, "dom", dom, 2 * k) for k in range(1, pairs)]
        odd = [swap(message, "dom", dom, 1)]

        tables = phase_tables()
        *angles, pieces[0] = call(
            lambda *r: table_body(*r, width=width),
            [shape(tables.shape[1:], F32)] * 2 + [shape(particles.shape, BF16)],
            "tables",
        )(where, tables, particles)

        *moved, moved_rest = call(
            lambda *r: shift_body(*r, parts=cls, pairs=pairs, width=width),
            [pltpu.VMEM((MAIN * rows, 2 * width), BF16)] * pairs + [shape((rows, F), BF16)],
            "shift",
            limit=4,
            scratch=[pltpu.VMEM((rows, F), F32)] * 2,
        )(where, *pieces, *angles)

        held = pltpu.VMEM((MAIN * rows, 2 * width), BF16)
        partial = []
        for j in range(pairs):
            last = j == pairs - 1
            rest = [k for k in range(pairs) if k != j]
            first_held = 4 if last else 3
            first_other = 4 + len(partial)
            aliases = {2: first_held + j}
            aliases |= {first_other + n: first_held + k for n, k in enumerate(rest)}
            if partial:
                aliases |= {4: 0, 5: 1}
            body = last_stage_body if last else stage_body
            options = {} if last else {"first": not partial}
            outs = [pltpu.VMEM((STEPS, h, block), F32), shape((h, rows), F32)]
            scratch = [pltpu.VMEM((h, 2 * width), BF16)]
            if last:
                outs += [shape((STEPS + 1, 8, block), F32), shape((8, 128), F32)]
                scratch += [
                    pltpu.VMEM((h, 128), F32),
                    pltpu.VMEM((h, block), F32),
                    pltpu.VMEM((h, block), F32),
                    pltpu.VMEM((STEPS, 8, block), F32),
                ]
            else:
                outs += [shape((8, length), F32)]
            if not last:
                if partial:
                    partial[2], even[j + 1] = lax.optimization_barrier((partial[2], even[j + 1]))
                else:
                    moved_rest, even[j + 1] = lax.optimization_barrier((moved_rest, even[j + 1]))
                odd.append(swap(even[j + 1], "dom", dom, 1))
            results = call(
                lambda *r: body(
                    *r, others=pairs - 1, length=length, rest_at=2 * j * width, **options
                ),
                outs + [held] * pairs,
                "score",
                scratch,
                limit=7 if last else 4,
                aliases=aliases,
            )(even[j], odd[j], moved[j], moved_rest, *partial, *[moved[k] for k in rest])
            partial, moved = list(results[:first_held]), results[first_held:]
        weights, weights_rest, tops, stats = partial

        gathered = [stats] + [swap(stats, "cls", cls, k) for k in range(1, cls)]

        accumulator = pltpu.VMEM((h, 2 * width), F32)
        order = list(range(pairs - 1, -1, -1))
        messages = []
        probs, probs_rest, own, other, weight_row, *kept = call(
            lambda *r: first_sums_body(
                *r, groups=cls, others=pairs - 1, length=length, rest_at=order[0] * 2 * width
            ),
            [
                shape((STEPS, h, block), BF16),
                shape((h, rows), BF16),
                shape((h, width), F32),
                shape((h + TAIL, width), BF16),
                shape((8, length), F32),
            ]
            + [pltpu.VMEM((MAIN * rows, 2 * width), BF16)] * (pairs - 1),
            "sums_first",
            aliases={cls + 5 + k: 5 + k for k in range(pairs - 1)},
            limit=4,
            scratch=[
                accumulator,
                pltpu.VMEM((8, block), F32),
                pltpu.VMEM((8, block), F32),
                pltpu.VMEM(tops.shape, F32),
                pltpu.VMEM((h, 128), F32),
                pltpu.VMEM((length, 128), F32),
                pltpu.VMEM((TAIL, width), F32),
            ],
        )(*gathered, weights, weights_rest, tops, moved[order[0]], moved_rest, *moved[:-1])
        received = swap(other, "dom", dom, 1)
        first, chip_row = call(
            first_pair_body,
            [shape((h + TAIL, width), BF16), shape((8, length), F32)],
            "pair_first",
            [pltpu.VMEM((TAIL, width), F32)],
        )(own, received, weight_row)
        messages.append(swap(first, "dom", dom, 2 * order[0]))
        ready = first

        for n, k in enumerate(order[1:]):
            if not k:
                probs_rest, messages[0] = lax.optimization_barrier((probs_rest, messages[0]))
            elif n:
                probs_rest, ready = lax.optimization_barrier((probs_rest, ready))
            own, other, *kept = call(
                lambda *r: sums_body(*r, others=k, rest_at=k * 2 * width),
                [shape((h, width), F32), shape((h, width), BF16)]
                + [pltpu.VMEM((MAIN * rows, 2 * width), BF16)] * k,
                "sums",
                [accumulator],
                aliases={4 + j: 2 + j for j in range(k)},
            )(probs, probs_rest, kept[k], moved_rest, *kept[:k])
            received = swap(other, "dom", dom, 1)
            if k:
                (summed,) = call(pair_body, [shape((h + TAIL, width), BF16)], "pair")(
                    own, received, first
                )
                messages.append(swap(summed, "dom", dom, 2 * k))
                ready = summed

        sums, class_weight = call(
            lambda *r: finish_body(*r, count=len(messages)),
            [shape((h, width), F32), shape((classes, rotations), F32)],
            "finish",
        )(*messages, own, received, chip_row)
        return sums.reshape(rotations, classes, width).transpose(1, 0, 2), class_weight

    return on_device


def solution(mesh):
    return jax.shard_map(
        make_on_device(mesh.shape["dom"], mesh.shape["cls"]),
        mesh=mesh,
        in_specs=(P("dom", "cls"), P("cls", None, "dom"), P()),
        out_specs=(P("cls", None, "dom"), P("cls", None)),
        check_vma=False,
    )
```

```python
import math

import jax
import jax.numpy as jnp
import numpy as np
from jax import lax
from jax.experimental import pallas as pl
from jax.experimental.pallas import tpu as pltpu
from jax.sharding import PartitionSpec as P

WIN = 32
BOX = 64
SHIFT_SIDE = 9
SHIFTS = SHIFT_SIDE * SHIFT_SIDE
HALF = WIN * WIN
F = 2 * HALF
GROUP = 8
MAIN = SHIFTS // GROUP * GROUP
STEPS = MAIN // GROUP
TAIL = 16
F32 = jnp.float32
BF16 = jnp.bfloat16


def phase_tables():
    freq = np.arange(HALF)
    fy = freq // WIN - WIN // 2
    fx = freq % WIN - WIN // 2
    offset = np.arange(MAIN // 2)
    sy = offset // SHIFT_SIDE - SHIFT_SIDE // 2
    sx = offset % SHIFT_SIDE - SHIFT_SIDE // 2
    turns = sx[:, None] * fx[None, :] + sy[:, None] * fy[None, :]
    theta = (2.0 * math.pi / BOX) * turns
    return np.stack([np.cos(theta), np.sin(theta)]).astype(np.float32)


def contract(x, y, dims):
    return lax.dot_general(x, y, (dims, ((), ())), preferred_element_type=F32)


def spread(row):
    high = row.astype(BF16).astype(F32)
    rest = row - high
    mid = rest.astype(BF16).astype(F32)
    low = (rest - mid).astype(BF16).astype(F32)
    return high, mid, low


def column_to_row(column, length, scratch):
    h = column.shape[0]
    scratch[...] = jnp.zeros(scratch.shape, F32)
    scratch[0:h, :] = jnp.broadcast_to(column, (h, 128))
    return scratch[...].T[0:1, :]


def tail_block(row, width, scratch):
    scratch[...] = jnp.zeros(scratch.shape, F32)
    per = row.shape[1] // width
    for p, part in enumerate(spread(row)):
        for j in range(per):
            r = p * per + j
            scratch[r : r + 1, :] = part[:, j * width : (j + 1) * width]
    return scratch[...].astype(BF16)


def row_of_tail(tail, width, length):
    per = length // width
    pieces = []
    for j in range(per):
        rows = [tail[p * per + j : p * per + j + 1, :] for p in range(3)]
        pieces.append((rows[2] + rows[1]) + rows[0])
    return jnp.concatenate(pieces, axis=1) if per > 1 else pieces[0]


def begin_body(where, *refs, width):
    sources = refs[:4]
    message, cosine, sine, kept, x_ref, noise, tables, tall, tail, arrived = refs[4:]
    copies = [
        pltpu.make_async_copy(source, target, arrived.at[n])
        for n, (source, target) in enumerate(zip(sources, (x_ref, noise, tables, kept)))
    ]
    for copy in copies:
        copy.start()
    count = HALF // width
    at = pl.multiple_of(jnp.bitwise_and(where[0], count - 1) * width, 128)
    h = x_ref.shape[0]
    copies[0].wait()
    copies[1].wait()
    x = x_ref[...]
    w = noise[:, pl.ds(at, width)]
    message[0:h, :] = (x * w).astype(BF16)
    half = 0.5 * jnp.sum(x * x * w, axis=1, keepdims=True)
    row = column_to_row(half, tall.shape[0], tall)
    message[h : h + TAIL, :] = tail_block(row, width, tail)
    copies[2].wait()
    sign = jnp.where(where[0] < count, 1.0, -1.0).astype(F32)
    for k in range(count):
        at = pl.multiple_of(jnp.bitwise_and(jnp.bitwise_xor(where[0], k), count - 1) * width, 128)
        cosine[:, k * width : (k + 1) * width] = tables[0, :, pl.ds(at, width)]
        sine[:, k * width : (k + 1) * width] = tables[1, :, pl.ds(at, width)] * sign
    copies[3].wait()


def shift_body(where, *refs, parts, pairs, width):
    pieces = refs[:parts]
    cosine, sine = refs[parts : parts + 2]
    outs = refs[parts + 2 : parts + 2 + pairs]
    rest, plain, whole = refs[parts + 2 + pairs :]
    rows, part_width = pieces[0].shape
    for k in range(parts):
        at = pl.multiple_of(jnp.bitwise_xor(where[2], k) * part_width, 128)
        plain[:, pl.ds(at, part_width)] = pieces[k][...].astype(F32)
    for k in range(2 * pairs):
        at = pl.multiple_of(jnp.bitwise_xor(where[0], k) * width, 128)
        whole[:, k * width : (k + 1) * width] = plain[:, pl.ds(at, width)]
    rest[...] = whole[...].astype(BF16)

    def one(s, carry):
        at = pl.multiple_of(2 * s * rows, rows)
        back = pl.multiple_of((2 * s + 1) * rows, rows)
        c_all = cosine[pl.ds(s, 1), :]
        s_all = sine[pl.ds(s, 1), :]
        for k in range(pairs):
            q = k * width
            c_row = c_all[:, q : q + width]
            s_row = s_all[:, q : q + width]
            a = whole[:, q : q + width]
            b = whole[:, HALF + q : HALF + q + width]
            ac, bs, bc, sa = a * c_row, b * s_row, b * c_row, a * s_row
            low = slice((k % 2) * width, (k % 2 + 1) * width)
            outs[k // 2][pl.ds(at, rows), low] = (ac + bs).astype(BF16)
            outs[(k + pairs) // 2][pl.ds(at, rows), low] = (bc - sa).astype(BF16)
            outs[k // 2][pl.ds(back, rows), low] = (ac - bs).astype(BF16)
            outs[(k + pairs) // 2][pl.ds(back, rows), low] = (bc + sa).astype(BF16)
        return carry

    lax.fori_loop(0, MAIN // 2, one, 0)


def load_slabs(slabs, weighted, row, length):
    h = weighted.shape[0]
    width = slabs[0].shape[1]
    for k, slab in enumerate(slabs):
        weighted[:, k * width : (k + 1) * width] = slab[0:h, :]
        row += row_of_tail(slab[h : h + TAIL, :].astype(F32), width, length)
    return row


def stage_body(*refs, first, count, others, length, rest_at):
    slabs, moved, moved_rest = refs[: 2 * count], refs[2 * count : 3 * count], refs[3 * count]
    at = 3 * count + 1
    partial = None if first else refs[at : at + 3]
    at += (0 if first else 3) + others
    scores, scores_rest, norms = refs[at : at + 3]
    weighted = refs[-1]
    span = weighted.shape[1]
    block = scores.shape[2]
    row = jnp.zeros((1, length), F32) if first else partial[2][0:1, :]
    norms[...] = jnp.broadcast_to(load_slabs(slabs, weighted, row, length), norms.shape)
    last = contract(weighted[...], moved_rest[:, rest_at : rest_at + span], ((1,), (1,)))
    scores_rest[...] = last if first else partial[1][...] + last
    for i in range(STEPS):
        x = jnp.concatenate([m[i * block : (i + 1) * block, :] for m in moved], axis=1)
        x = contract(weighted[...], x, ((1,), (1,)))
        scores[i] = x if first else partial[0][i] + x


def last_stage_body(*refs, count, others, length, rest_at):
    slabs, moved, moved_rest = refs[: 2 * count], refs[2 * count : 3 * count], refs[3 * count]
    scores, scores_rest, norms = refs[3 * count + 1 : 3 * count + 4]
    at = 3 * count + 4 + others
    weights, weights_rest, tops, stats = refs[at : at + 4]
    weighted, half, even, odd, totals = refs[-5:]
    h, block = even.shape
    rows = moved_rest.shape[0]
    span = weighted.shape[1]
    row = load_slabs(slabs, weighted, norms[0:1, :], length)
    half[...] = jnp.broadcast_to(row, (128, length)).T[0:h, :]

    def multiply(i, target):
        x = jnp.concatenate([m[i * block : (i + 1) * block, :] for m in moved], axis=1)
        target[...] = scores[i] + contract(weighted[...], x, ((1,), (1,)))

    def soften(i, source):
        for q in range(0, block, 128):
            x = source[:, q : q + 128] - half[...]
            top = jnp.max(x, axis=0, keepdims=True)
            x = jnp.exp(x - top)
            weights[i, :, q : q + 128] = x
            tops[i, :, q : q + 128] = jnp.broadcast_to(top, (8, 128))
            total = jnp.sum(x, axis=0, keepdims=True)
            totals[i, :, q : q + 128] = jnp.broadcast_to(total, (8, 128))

    multiply(0, even)
    for i in range(1, STEPS):
        multiply(i, odd if i % 2 else even)
        soften(i - 1, even if i % 2 else odd)
    last = contract(weighted[...], moved_rest[:, rest_at : rest_at + span], ((1,), (1,)))
    last = scores_rest[...] + last - half[:, 0:1]
    soften(STEPS - 1, odd if (STEPS - 1) % 2 else even)

    best = jnp.max(last, axis=0, keepdims=True)
    last = jnp.exp(last - best)
    weights_rest[...] = last
    tops[STEPS, 0:1, 0:rows] = best
    mass = jnp.sum(last, axis=0, keepdims=True)
    lane_top = tops[0]
    for i in range(1, STEPS):
        lane_top = jnp.maximum(lane_top, tops[i])
    lane_mass = totals[0] * jnp.exp(tops[0] - lane_top)
    for i in range(1, STEPS):
        lane_mass += totals[i] * jnp.exp(tops[i] - lane_top)
    parts_top = [lane_top[0:1, j * rows : (j + 1) * rows] for j in range(GROUP)]
    peak = best
    for t in parts_top:
        peak = jnp.maximum(peak, t)
    mass = mass * jnp.exp(best - peak)
    for j in range(GROUP):
        mass += lane_mass[0:1, j * rows : (j + 1) * rows] * jnp.exp(parts_top[j] - peak)
    stats[...] = jnp.zeros(stats.shape, F32)
    stats[0:1, 0:rows] = peak
    stats[1:2, 0:rows] = mass


def split_pair(sums, own, other):
    h, width = own.shape
    own[...] = sums[:, 0:width]
    other[0:h, :] = sums[:, width : 2 * width].astype(BF16)


def accumulate(sums, probs, probs_rest, moved, moved_rest, rest_at, ahead=None):
    block = probs.shape[2]
    if ahead:
        ahead(0)
    sums[...] = contract(probs_rest[...], moved_rest[:, rest_at : rest_at + sums.shape[1]], ((1,), (0,)))
    for i in range(STEPS):
        if ahead and i + 1 < STEPS:
            ahead(i + 1)
        sums[...] += contract(probs[i], moved[i * block : (i + 1) * block, :], ((1,), (0,)))


def first_sums_body(*refs, groups, others, length, rest_at):
    gathered = refs[:groups]
    weights, weights_rest, tops, moved, moved_rest = refs[groups : groups + 5]
    probs, probs_rest, own, other, weight_row = refs[groups + 5 + others : groups + 10 + others]
    sums, peak, inverse, scale, mass, tall, tail = refs[-7:]
    h, width = own.shape
    rows = moved_rest.shape[0]
    block = probs.shape[2]

    best = gathered[0][0:1, 0:rows]
    for g in gathered[1:]:
        best = jnp.maximum(best, g[0:1, 0:rows])
    whole = jnp.zeros((1, rows), F32)
    for g in gathered:
        whole += g[1:2, 0:rows] * jnp.exp(g[0:1, 0:rows] - best)
    over = 1.0 / whole
    for j in range(GROUP):
        peak[:, j * rows : (j + 1) * rows] = jnp.broadcast_to(best, (8, rows))
        inverse[:, j * rows : (j + 1) * rows] = jnp.broadcast_to(over, (8, rows))
    for i in range(STEPS):
        scale[i] = jnp.exp(tops[i] - peak[...]) * inverse[...]

    last = weights_rest[...] * (jnp.exp(tops[STEPS, 0:1, 0:rows] - best) * over)
    last_low = last.astype(BF16)
    probs_rest[...] = last_low
    mass[...] = jnp.zeros(mass.shape, F32)
    mass[:, 0:1] = jnp.sum(last, axis=1, keepdims=True)

    def normalise(i):
        part = mass[...]
        for q in range(0, block, 128):
            prob = weights[i, :, q : q + 128] * scale[i, 0:1, q : q + 128]
            probs[i, :, q : q + 128] = prob.astype(BF16)
            part += prob
        mass[...] = part

    accumulate(sums, probs, probs_rest, moved, moved_rest, rest_at, normalise)
    split_pair(sums, own, other)
    row = column_to_row(jnp.sum(mass[...], axis=1, keepdims=True), length, tall)
    weight_row[...] = jnp.broadcast_to(row, weight_row.shape)
    other[h : h + TAIL, :] = tail_block(row, width, tail)


def sums_body(probs, probs_rest, moved, moved_rest, *refs, others, rest_at):
    own, other = refs[others : others + 2]
    sums = refs[-1]
    accumulate(sums, probs, probs_rest, moved, moved_rest, rest_at)
    split_pair(sums, own, other)


def first_pair_body(own, received, weight_row, message, chip_row, tail):
    h, width = own.shape
    message[0:h, :] = (own[...] + received[0:h, :].astype(F32)).astype(BF16)
    length = weight_row.shape[1]
    row = weight_row[0:1, :] + row_of_tail(received[h : h + TAIL, :].astype(F32), width, length)
    chip_row[...] = jnp.broadcast_to(row, chip_row.shape)
    message[h : h + TAIL, :] = tail_block(row, width, tail)


def pair_body(own, received, chip_row, *refs):
    arrived = refs[:-2]
    message, tail = refs[-2:]
    h, width = own.shape
    length = chip_row.shape[1]
    x = own[...] + received[...].astype(F32)
    row = chip_row[0:1, :]
    for m in arrived:
        x += m[0:h, :].astype(F32)
        row += row_of_tail(m[h : h + TAIL, :].astype(F32), width, length)
    message[0:h, :] = x.astype(BF16)
    message[h : h + TAIL, :] = tail_block(row, width, tail)


def finish_body(*refs, count):
    messages = refs[:count]
    own, received, chip_row, class_sums, class_weight = refs[count:]
    h, width = own.shape
    rotations, classes = class_weight.shape[1], class_weight.shape[0]
    length = chip_row.shape[1]
    x = own[...] + received[...].astype(F32)
    row = chip_row[0:1, :]
    for m in messages:
        x += m[0:h, :].astype(F32)
        row += row_of_tail(m[h : h + TAIL, :].astype(F32), width, length)
    class_sums[...] = x
    shape = (classes, length)
    at = lax.broadcasted_iota(jnp.int32, shape, 1)
    mine = at - at // classes * classes == lax.broadcasted_iota(jnp.int32, shape, 0)
    spread_out = jnp.where(mine, jnp.broadcast_to(row, shape), 0.0)
    shape = (length, rotations)
    pick = lax.broadcasted_iota(jnp.int32, shape, 0) // classes == lax.broadcasted_iota(
        jnp.int32, shape, 1
    )
    class_weight[...] = lax.dot_general(
        spread_out,
        pick.astype(F32),
        (((1,), (0,)), ((), ())),
        precision=lax.Precision.HIGHEST,
        preferred_element_type=F32,
    )


VMEM = pl.BlockSpec(memory_space=pltpu.VMEM)


def make_on_device(dom, cls):
    pairs = dom // 2

    def swap(x, axis, size, k):
        return lax.ppermute(x, axis, [(i, i ^ k) for i in range(size)])

    def on_device(particles, references, noise_weight):
        rows, part_width = particles.shape
        classes, rotations, width = references.shape
        h = classes * rotations
        length = -(-h // width) * width
        block = GROUP * rows
        shape = jax.ShapeDtypeStruct
        place = lax.axis_index("dom")
        where = jnp.stack([place, place % 2, lax.axis_index("cls")]).astype(jnp.int32)

        def call(body, shapes, name, scratch=(), limit=2, aliases=None, inputs=VMEM, flops=1):
            def run(*args):
                scalars = args[0] is where
                specs = [inputs] * (len(args) - scalars)
                spec = pltpu.PrefetchScalarGridSpec(
                    num_scalar_prefetch=int(scalars),
                    grid=(),
                    in_specs=specs,
                    out_specs=[VMEM] * len(shapes),
                    scratch_shapes=list(scratch),
                )
                params = pltpu.CompilerParams(vmem_limit_bytes=limit * 1024 * 1024)
                return pl.pallas_call(
                    body,
                    grid_spec=spec,
                    out_shape=shapes,
                    compiler_params=params,
                    input_output_aliases=aliases or {},
                    cost_estimate=pl.CostEstimate(flops=flops, transcendentals=0, bytes_accessed=1),
                    name=name,
                )(*args)

            return run

        pieces = [particles] + [swap(particles, "cls", cls, k) for k in range(1, cls)]

        tables = phase_tables()
        ref_rows = references.transpose(1, 0, 2).reshape(h, width)
        message, *angles, pieces[0] = call(
            lambda *r: begin_body(*r, width=width),
            [shape((h + TAIL, width), BF16)]
            + [shape(tables.shape[1:], F32)] * 2
            + [shape(particles.shape, BF16)],
            "begin",
            [
                pltpu.VMEM((h, width), F32),
                pltpu.VMEM((1, HALF), F32),
                pltpu.VMEM(tables.shape, F32),
                pltpu.VMEM((length, 128), F32),
                pltpu.VMEM((TAIL, width), F32),
                pltpu.SemaphoreType.DMA((4,)),
            ],
            inputs=pl.BlockSpec(memory_space=pltpu.HBM),
        )(
            where,
            *[
                pltpu.with_memory_space_constraint(x, pltpu.HBM)
                for x in (ref_rows, noise_weight.reshape(1, HALF), jnp.asarray(tables), particles)
            ],
        )

        even = [message] + [swap(message, "dom", dom, 2 * k) for k in range(1, pairs)]
        odd = [swap(message, "dom", dom, 1)]

        *moved, moved_rest = call(
            lambda *r: shift_body(*r, parts=cls, pairs=pairs, width=width),
            [pltpu.VMEM((MAIN * rows, 2 * width), BF16)] * pairs + [shape((rows, F), BF16)],
            "shift",
            flops=10**10,
            limit=2,
            scratch=[pltpu.VMEM((rows, F), F32)] * 2,
        )(where, *pieces, *angles)

        held = pltpu.VMEM((MAIN * rows, 2 * width), BF16)
        partial = []
        stages = [[0]] + [list(range(1 << t, 2 << t)) for t in range((pairs - 1).bit_length())]
        for n, stage in enumerate(stages):
            last = stage[-1] == pairs - 1
            count = len(stage)
            rest = [k for k in range(pairs) if k not in stage]
            first_held = 4 if last else 3
            after = 3 * count + 1 + len(partial)
            aliases = {2 * count + m: first_held + k for m, k in enumerate(stage)}
            aliases |= {after + m: first_held + k for m, k in enumerate(rest)}
            if partial:
                aliases |= {3 * count + 1: 0, 3 * count + 2: 1}
            body = last_stage_body if last else stage_body
            options = {} if last else {"first": not partial}
            outs = [pltpu.VMEM((STEPS, h, block), F32), shape((h, rows), F32)]
            scratch = [pltpu.VMEM((h, 2 * width * count), BF16)]
            if last:
                outs += [shape((STEPS + 1, 8, block), F32), shape((8, 128), F32)]
                scratch += [
                    pltpu.VMEM((h, 128), F32),
                    pltpu.VMEM((h, block), F32),
                    pltpu.VMEM((h, block), F32),
                    pltpu.VMEM((STEPS, 8, block), F32),
                ]
            else:
                outs += [shape((8, length), F32)]
                for k in stages[n + 1]:
                    if partial:
                        partial[2], even[k] = lax.optimization_barrier((partial[2], even[k]))
                    else:
                        moved_rest, even[k] = lax.optimization_barrier((moved_rest, even[k]))
                    odd.append(swap(even[k], "dom", dom, 1))
            results = call(
                lambda *r: body(
                    *r,
                    count=count,
                    others=len(rest),
                    length=length,
                    rest_at=2 * stage[0] * width,
                    **options,
                ),
                outs + [held] * pairs,
                "score",
                scratch,
                limit=6 if last else 6,
                aliases=aliases,
            )(
                *[m for k in stage for m in (even[k], odd[k])],
                *[moved[k] for k in stage],
                moved_rest,
                *partial,
                *[moved[k] for k in rest],
            )
            partial, moved = list(results[:first_held]), results[first_held:]
        weights, weights_rest, tops, stats = partial

        gathered = [stats] + [swap(stats, "cls", cls, k) for k in range(1, cls)]

        accumulator = pltpu.VMEM((h, 2 * width), F32)
        order = sorted(range(1, pairs), key=lambda k: (k & -k, -k)) + [0]
        sent = {}

        def children(k):
            low = k & -k or pairs
            return [sent[k | 1 << t] for t in range(low.bit_length() - 1)]

        probs, probs_rest, own, other, weight_row, *kept = call(
            lambda *r: first_sums_body(
                *r, groups=cls, others=pairs - 1, length=length, rest_at=order[0] * 2 * width
            ),
            [
                shape((STEPS, h, block), BF16),
                shape((h, rows), BF16),
                shape((h, width), F32),
                shape((h + TAIL, width), BF16),
                shape((8, length), F32),
            ]
            + [held] * (pairs - 1),
            "sums_first",
            aliases={cls + 5 + k: 5 + k for k in range(pairs - 1)},
            limit=2,
            scratch=[
                accumulator,
                pltpu.VMEM((8, block), F32),
                pltpu.VMEM((8, block), F32),
                pltpu.VMEM(tops.shape, F32),
                pltpu.VMEM((h, 128), F32),
                pltpu.VMEM((length, 128), F32),
                pltpu.VMEM((TAIL, width), F32),
            ],
        )(
            *gathered,
            weights,
            weights_rest,
            tops,
            moved[order[0]],
            moved_rest,
            *[moved[k] for k in order[1:]],
        )
        received = swap(other, "dom", dom, 1)
        first, chip_row = call(
            first_pair_body,
            [shape((h + TAIL, width), BF16), shape((8, length), F32)],
            "pair_first",
            [pltpu.VMEM((TAIL, width), F32)],
        )(own, received, weight_row)
        sent[order[0]] = swap(first, "dom", dom, 2 * (order[0] & -order[0]))
        ready = first

        for n, k in enumerate(order[1:]):
            if n:
                probs_rest, ready = lax.optimization_barrier((probs_rest, ready))
            others = pairs - 2 - n
            own, other, *kept = call(
                lambda *r: sums_body(*r, others=others, rest_at=k * 2 * width),
                [shape((h, width), F32), shape((h, width), BF16)] + [held] * others,
                "sums",
                [accumulator],
                aliases={4 + j: 2 + j for j in range(others)},
            )(probs, probs_rest, kept[0], moved_rest, *kept[1:])
            received = swap(other, "dom", dom, 1)
            if k:
                (ready,) = call(
                    pair_body,
                    [shape((h + TAIL, width), BF16)],
                    "pair",
                    [pltpu.VMEM((TAIL, width), F32)],
                )(own, received, chip_row, *children(k))
                sent[k] = swap(ready, "dom", dom, 2 * (k & -k))

        arrived = children(0)
        sums, class_weight = call(
            lambda *r: finish_body(*r, count=len(arrived)),
            [shape((h, width), F32), shape((classes, rotations), F32)],
            "finish",
        )(*arrived, own, received, chip_row)
        return sums.reshape(rotations, classes, width).transpose(1, 0, 2), class_weight

    return on_device


def solution(mesh):
    return jax.shard_map(
        make_on_device(mesh.shape["dom"], mesh.shape["cls"]),
        mesh=mesh,
        in_specs=(P("dom", "cls"), P("cls", None, "dom"), P()),
        out_specs=(P("cls", None, "dom"), P("cls", None)),
        check_vma=False,
    )
```

```python
import math

import jax
import jax.numpy as jnp
import numpy as np
from jax import lax
from jax.experimental import pallas as pl
from jax.experimental.pallas import tpu as pltpu
from jax.sharding import PartitionSpec as P

WIN = 32
BOX = 64
SHIFT_SIDE = 9
SHIFTS = SHIFT_SIDE * SHIFT_SIDE
HALF = WIN * WIN
F = 2 * HALF
GROUP = 8
MAIN = SHIFTS // GROUP * GROUP
STEPS = MAIN // GROUP
TAIL = 8
F32 = jnp.float32
BF16 = jnp.bfloat16


def phase_tables():
    freq = np.arange(HALF)
    fy = freq // WIN - WIN // 2
    fx = freq % WIN - WIN // 2
    offset = np.arange(MAIN // 2)
    sy = offset // SHIFT_SIDE - SHIFT_SIDE // 2
    sx = offset % SHIFT_SIDE - SHIFT_SIDE // 2
    turns = sx[:, None] * fx[None, :] + sy[:, None] * fy[None, :]
    theta = (2.0 * math.pi / BOX) * turns
    return np.stack([np.cos(theta), np.sin(theta)]).astype(np.float32)


def contract(x, y, dims):
    return lax.dot_general(x, y, (dims, ((), ())), preferred_element_type=F32)


def spread(row):
    high = row.astype(BF16).astype(F32)
    rest = row - high
    mid = rest.astype(BF16).astype(F32)
    low = (rest - mid).astype(BF16).astype(F32)
    return high, mid, low


def column_to_row(column, length, scratch):
    h = column.shape[0]
    scratch[...] = jnp.zeros(scratch.shape, F32)
    scratch[0:h, :] = jnp.broadcast_to(column, (h, 128))
    return scratch[...].T[0:1, :]


def tail_block(row, width, scratch):
    scratch[...] = jnp.zeros(scratch.shape, F32)
    per = row.shape[1] // width
    for p, part in enumerate(spread(row)):
        for j in range(per):
            r = p * per + j
            scratch[r : r + 1, :] = part[:, j * width : (j + 1) * width]
    return scratch[...].astype(BF16)


def row_of_tail(tail, width, length):
    per = length // width
    pieces = []
    for j in range(per):
        rows = [tail[p * per + j : p * per + j + 1, :] for p in range(3)]
        pieces.append((rows[2] + rows[1]) + rows[0])
    return jnp.concatenate(pieces, axis=1) if per > 1 else pieces[0]


def begin_body(where, *refs, width):
    sources = refs[:4]
    message, cosine, sine, kept, x_ref, noise, tables, tall, tail, arrived = refs[4:]
    copies = [
        pltpu.make_async_copy(source, target, arrived.at[n])
        for n, (source, target) in enumerate(zip(sources, (x_ref, noise, tables, kept)))
    ]
    for copy in copies:
        copy.start()
    count = HALF // width
    at = pl.multiple_of(jnp.bitwise_and(where[0], count - 1) * width, 128)
    h = x_ref.shape[0]
    copies[0].wait()
    copies[1].wait()
    x = x_ref[...]
    w = noise[:, pl.ds(at, width)]
    message[0:h, :] = (x * w).astype(BF16)
    half = 0.5 * jnp.sum(x * x * w, axis=1, keepdims=True)
    row = column_to_row(half, tall.shape[0], tall)
    message[h : h + TAIL, :] = tail_block(row, width, tail)
    copies[2].wait()
    sign = jnp.where(where[0] < count, 1.0, -1.0).astype(F32)
    for k in range(count):
        at = pl.multiple_of(jnp.bitwise_and(jnp.bitwise_xor(where[0], k), count - 1) * width, 128)
        cosine[:, k * width : (k + 1) * width] = tables[0, :, pl.ds(at, width)]
        sine[:, k * width : (k + 1) * width] = tables[1, :, pl.ds(at, width)] * sign
    copies[3].wait()


def shift_body(where, *refs, parts, pairs, width):
    pieces = refs[:parts]
    cosine, sine = refs[parts : parts + 2]
    outs = refs[parts + 2 : parts + 2 + pairs]
    rest, plain, whole = refs[parts + 2 + pairs :]
    rows, part_width = pieces[0].shape
    for k in range(parts):
        at = pl.multiple_of(jnp.bitwise_xor(where[2], k) * part_width, 128)
        plain[:, pl.ds(at, part_width)] = pieces[k][...].astype(F32)
    for k in range(2 * pairs):
        at = pl.multiple_of(jnp.bitwise_xor(where[0], k) * width, 128)
        whole[:, k * width : (k + 1) * width] = plain[:, pl.ds(at, width)]
    rest[...] = whole[...].astype(BF16)

    def one(s, carry):
        at = pl.multiple_of(2 * s * rows, rows)
        back = pl.multiple_of((2 * s + 1) * rows, rows)
        c_all = cosine[pl.ds(s, 1), :]
        s_all = sine[pl.ds(s, 1), :]
        for k in range(pairs):
            q = k * width
            c_row = c_all[:, q : q + width]
            s_row = s_all[:, q : q + width]
            a = whole[:, q : q + width]
            b = whole[:, HALF + q : HALF + q + width]
            ac, bs, bc, sa = a * c_row, b * s_row, b * c_row, a * s_row
            low = slice((k % 2) * width, (k % 2 + 1) * width)
            outs[k // 2][pl.ds(at, rows), low] = (ac + bs).astype(BF16)
            outs[(k + pairs) // 2][pl.ds(at, rows), low] = (bc - sa).astype(BF16)
            outs[k // 2][pl.ds(back, rows), low] = (ac - bs).astype(BF16)
            outs[(k + pairs) // 2][pl.ds(back, rows), low] = (bc + sa).astype(BF16)
        return carry

    lax.fori_loop(0, MAIN // 2, one, 0)


def load_slabs(slabs, weighted, row, length):
    h = weighted.shape[0]
    width = slabs[0].shape[1]
    for k, slab in enumerate(slabs):
        weighted[:, k * width : (k + 1) * width] = slab[0:h, :]
        row += row_of_tail(slab[h : h + TAIL, :].astype(F32), width, length)
    return row


def stage_body(*refs, first, count, others, length, rest_at):
    slabs, moved, moved_rest = refs[: 2 * count], refs[2 * count : 3 * count], refs[3 * count]
    at = 3 * count + 1
    partial = None if first else refs[at : at + 3]
    at += (0 if first else 3) + others
    scores, scores_rest, norms = refs[at : at + 3]
    weighted = refs[-1]
    span = weighted.shape[1]
    block = scores.shape[2]
    row = jnp.zeros((1, length), F32) if first else partial[2][0:1, :]
    norms[...] = jnp.broadcast_to(load_slabs(slabs, weighted, row, length), norms.shape)
    last = contract(weighted[...], moved_rest[:, rest_at : rest_at + span], ((1,), (1,)))
    scores_rest[...] = last if first else partial[1][...] + last
    for i in range(STEPS):
        x = jnp.concatenate([m[i * block : (i + 1) * block, :] for m in moved], axis=1)
        x = contract(weighted[...], x, ((1,), (1,)))
        scores[i] = x if first else partial[0][i] + x


def last_stage_body(*refs, count, others, length, rest_at):
    slabs, moved, moved_rest = refs[: 2 * count], refs[2 * count : 3 * count], refs[3 * count]
    scores, scores_rest, norms = refs[3 * count + 1 : 3 * count + 4]
    at = 3 * count + 4 + others
    weights, weights_rest, tops, stats = refs[at : at + 4]
    weighted, half, even, odd, totals = refs[-5:]
    h, block = even.shape
    rows = moved_rest.shape[0]
    span = weighted.shape[1]
    row = load_slabs(slabs, weighted, norms[0:1, :], length)
    half[...] = jnp.broadcast_to(row, (128, length)).T[0:h, :]

    def multiply(i, target):
        x = jnp.concatenate([m[i * block : (i + 1) * block, :] for m in moved], axis=1)
        target[...] = scores[i] + contract(weighted[...], x, ((1,), (1,)))

    def soften(i, source):
        for q in range(0, block, 128):
            x = source[:, q : q + 128] - half[...]
            top = jnp.max(x, axis=0, keepdims=True)
            x = jnp.exp(x - top)
            weights[i, :, q : q + 128] = x
            tops[i, :, q : q + 128] = jnp.broadcast_to(top, (8, 128))
            total = jnp.sum(x, axis=0, keepdims=True)
            totals[i, :, q : q + 128] = jnp.broadcast_to(total, (8, 128))

    multiply(0, even)
    for i in range(1, STEPS):
        multiply(i, odd if i % 2 else even)
        soften(i - 1, even if i % 2 else odd)
    last = contract(weighted[...], moved_rest[:, rest_at : rest_at + span], ((1,), (1,)))
    last = scores_rest[...] + last - half[:, 0:1]
    soften(STEPS - 1, odd if (STEPS - 1) % 2 else even)

    best = jnp.max(last, axis=0, keepdims=True)
    last = jnp.exp(last - best)
    weights_rest[...] = last
    tops[STEPS, 0:1, 0:rows] = best
    mass = jnp.sum(last, axis=0, keepdims=True)
    lane_top = tops[0]
    for i in range(1, STEPS):
        lane_top = jnp.maximum(lane_top, tops[i])
    lane_mass = totals[0] * jnp.exp(tops[0] - lane_top)
    for i in range(1, STEPS):
        lane_mass += totals[i] * jnp.exp(tops[i] - lane_top)
    parts_top = [lane_top[0:1, j * rows : (j + 1) * rows] for j in range(GROUP)]
    peak = best
    for t in parts_top:
        peak = jnp.maximum(peak, t)
    mass = mass * jnp.exp(best - peak)
    for j in range(GROUP):
        mass += lane_mass[0:1, j * rows : (j + 1) * rows] * jnp.exp(parts_top[j] - peak)
    stats[...] = jnp.zeros(stats.shape, F32)
    stats[0:1, 0:rows] = peak
    stats[1:2, 0:rows] = mass


def split_pair(sums, own, other):
    h, width = own.shape
    own[...] = sums[:, 0:width]
    other[0:h, :] = sums[:, width : 2 * width].astype(BF16)


def accumulate(sums, probs, probs_rest, moved, moved_rest, rest_at, ahead=None):
    block = probs.shape[2]
    if ahead:
        ahead(0)
    sums[...] = contract(probs_rest[...], moved_rest[:, rest_at : rest_at + sums.shape[1]], ((1,), (0,)))
    for i in range(STEPS):
        sums[...] += contract(probs[i], moved[i * block : (i + 1) * block, :], ((1,), (0,)))
        if ahead and i + 1 < STEPS:
            ahead(i + 1)


def first_sums_body(*refs, groups, others, length, rest_at):
    gathered = refs[:groups]
    weights, weights_rest, tops, moved, moved_rest = refs[groups : groups + 5]
    probs, probs_rest, own, other, weight_row = refs[groups + 5 + others : groups + 10 + others]
    sums, peak, inverse, scale, mass, tall, tail = refs[-7:]
    h, width = own.shape
    rows = moved_rest.shape[0]
    block = probs.shape[2]

    best = gathered[0][0:1, 0:rows]
    for g in gathered[1:]:
        best = jnp.maximum(best, g[0:1, 0:rows])
    whole = jnp.zeros((1, rows), F32)
    for g in gathered:
        whole += g[1:2, 0:rows] * jnp.exp(g[0:1, 0:rows] - best)
    over = 1.0 / whole
    for j in range(GROUP):
        peak[:, j * rows : (j + 1) * rows] = jnp.broadcast_to(best, (8, rows))
        inverse[:, j * rows : (j + 1) * rows] = jnp.broadcast_to(over, (8, rows))
    for i in range(STEPS):
        scale[i] = jnp.exp(tops[i] - peak[...]) * inverse[...]

    last = weights_rest[...] * (jnp.exp(tops[STEPS, 0:1, 0:rows] - best) * over)
    last_low = last.astype(BF16)
    probs_rest[...] = last_low
    mass[...] = jnp.zeros(mass.shape, F32)
    mass[:, 0:1] = jnp.sum(last, axis=1, keepdims=True)

    def normalise(i):
        part = mass[...]
        for q in range(0, block, 128):
            prob = weights[i, :, q : q + 128] * scale[i, 0:1, q : q + 128]
            probs[i, :, q : q + 128] = prob.astype(BF16)
            part += prob
        mass[...] = part

    accumulate(sums, probs, probs_rest, moved, moved_rest, rest_at, normalise)
    split_pair(sums, own, other)
    row = column_to_row(jnp.sum(mass[...], axis=1, keepdims=True), length, tall)
    weight_row[...] = jnp.broadcast_to(row, weight_row.shape)
    other[h : h + TAIL, :] = tail_block(row, width, tail)


def sums_body(probs, probs_rest, moved, moved_rest, *refs, others, rest_at):
    own, other = refs[others : others + 2]
    sums = refs[-1]
    accumulate(sums, probs, probs_rest, moved, moved_rest, rest_at)
    split_pair(sums, own, other)


def first_pair_body(own, received, weight_row, message, chip_row, tail):
    h, width = own.shape
    message[0:h, :] = (own[...] + received[0:h, :].astype(F32)).astype(BF16)
    length = weight_row.shape[1]
    row = weight_row[0:1, :] + row_of_tail(received[h : h + TAIL, :].astype(F32), width, length)
    chip_row[...] = jnp.broadcast_to(row, chip_row.shape)
    message[h : h + TAIL, :] = tail_block(row, width, tail)


def pair_body(own, received, chip_row, *refs):
    arrived = refs[:-2]
    message, tail = refs[-2:]
    h, width = own.shape
    length = chip_row.shape[1]
    x = own[...] + received[...].astype(F32)
    row = chip_row[0:1, :]
    for m in arrived:
        x += m[0:h, :].astype(F32)
        row += row_of_tail(m[h : h + TAIL, :].astype(F32), width, length)
    message[0:h, :] = x.astype(BF16)
    message[h : h + TAIL, :] = tail_block(row, width, tail)


def finish_body(*refs, count):
    messages = refs[:count]
    own, received, chip_row, class_sums, class_weight = refs[count:]
    h, width = own.shape
    rotations, classes = class_weight.shape[1], class_weight.shape[0]
    length = chip_row.shape[1]
    x = own[...] + received[...].astype(F32)
    row = chip_row[0:1, :]
    for m in messages:
        x += m[0:h, :].astype(F32)
        row += row_of_tail(m[h : h + TAIL, :].astype(F32), width, length)
    class_sums[...] = x
    shape = (classes, length)
    at = lax.broadcasted_iota(jnp.int32, shape, 1)
    mine = at - at // classes * classes == lax.broadcasted_iota(jnp.int32, shape, 0)
    spread_out = jnp.where(mine, jnp.broadcast_to(row, shape), 0.0)
    shape = (length, rotations)
    pick = lax.broadcasted_iota(jnp.int32, shape, 0) // classes == lax.broadcasted_iota(
        jnp.int32, shape, 1
    )
    class_weight[...] = lax.dot_general(
        spread_out,
        pick.astype(F32),
        (((1,), (0,)), ((), ())),
        precision=lax.Precision.HIGHEST,
        preferred_element_type=F32,
    )


VMEM = pl.BlockSpec(memory_space=pltpu.VMEM)


def make_on_device(dom, cls):
    pairs = dom // 2

    def swap(x, axis, size, k):
        return lax.ppermute(x, axis, [(i, i ^ k) for i in range(size)])

    def on_device(particles, references, noise_weight):
        rows, part_width = particles.shape
        classes, rotations, width = references.shape
        h = classes * rotations
        length = -(-h // width) * width
        block = GROUP * rows
        shape = jax.ShapeDtypeStruct
        place = lax.axis_index("dom")
        where = jnp.stack([place, place % 2, lax.axis_index("cls")]).astype(jnp.int32)

        def call(body, shapes, name, scratch=(), limit=2, aliases=None, inputs=VMEM, flops=1):
            def run(*args):
                scalars = args[0] is where
                specs = [inputs] * (len(args) - scalars)
                spec = pltpu.PrefetchScalarGridSpec(
                    num_scalar_prefetch=int(scalars),
                    grid=(),
                    in_specs=specs,
                    out_specs=[VMEM] * len(shapes),
                    scratch_shapes=list(scratch),
                )
                params = pltpu.CompilerParams(vmem_limit_bytes=limit * 1024 * 1024)
                return pl.pallas_call(
                    body,
                    grid_spec=spec,
                    out_shape=shapes,
                    compiler_params=params,
                    input_output_aliases=aliases or {},
                    cost_estimate=pl.CostEstimate(flops=flops, transcendentals=0, bytes_accessed=1),
                    name=name,
                )(*args)

            return run

        pieces = [particles] + [swap(particles, "cls", cls, k) for k in range(1, cls)]

        tables = phase_tables()
        ref_rows = references.transpose(1, 0, 2).reshape(h, width)
        message, *angles, pieces[0] = call(
            lambda *r: begin_body(*r, width=width),
            [shape((h + TAIL, width), BF16)]
            + [shape(tables.shape[1:], F32)] * 2
            + [shape(particles.shape, BF16)],
            "begin",
            [
                pltpu.VMEM((h, width), F32),
                pltpu.VMEM((1, HALF), F32),
                pltpu.VMEM(tables.shape, F32),
                pltpu.VMEM((length, 128), F32),
                pltpu.VMEM((TAIL, width), F32),
                pltpu.SemaphoreType.DMA((4,)),
            ],
            inputs=pl.BlockSpec(memory_space=pltpu.HBM),
        )(
            where,
            *[
                pltpu.with_memory_space_constraint(x, pltpu.HBM)
                for x in (ref_rows, noise_weight.reshape(1, HALF), jnp.asarray(tables), particles)
            ],
        )

        even = [message] + [None] * (pairs - 1)
        for k in range(1, pairs):
            if not k & (k - 1):
                even[k] = swap(message, "dom", dom, 2 * k)
        odd = [swap(message, "dom", dom, 1)]

        *moved, moved_rest = call(
            lambda *r: shift_body(*r, parts=cls, pairs=pairs, width=width),
            [pltpu.VMEM((MAIN * rows, 2 * width), BF16)] * pairs + [shape((rows, F), BF16)],
            "shift",
            flops=10**10,
            limit=2,
            scratch=[pltpu.VMEM((rows, F), F32)] * 2,
        )(where, *pieces, *angles)

        for k in range(1, pairs):
            if k & (k - 1):
                source = k & (k - 1)
                moved_rest, even[source] = lax.optimization_barrier((moved_rest, even[source]))
                even[k] = swap(even[source], "dom", dom, 2 * (k & -k))

        held = pltpu.VMEM((MAIN * rows, 2 * width), BF16)
        partial = []
        stages = [[0]] + [list(range(1 << t, 2 << t)) for t in range((pairs - 1).bit_length())]
        for n, stage in enumerate(stages):
            last = stage[-1] == pairs - 1
            count = len(stage)
            rest = [k for k in range(pairs) if k not in stage]
            first_held = 4 if last else 3
            after = 3 * count + 1 + len(partial)
            aliases = {2 * count + m: first_held + k for m, k in enumerate(stage)}
            aliases |= {after + m: first_held + k for m, k in enumerate(rest)}
            if partial:
                aliases |= {3 * count + 1: 0, 3 * count + 2: 1}
            body = last_stage_body if last else stage_body
            options = {} if last else {"first": not partial}
            outs = [pltpu.VMEM((STEPS, h, block), F32), shape((h, rows), F32)]
            scratch = [pltpu.VMEM((h, 2 * width * count), BF16)]
            if last:
                outs += [shape((STEPS + 1, 8, block), F32), shape((8, 128), F32)]
                scratch += [
                    pltpu.VMEM((h, 128), F32),
                    pltpu.VMEM((h, block), F32),
                    pltpu.VMEM((h, block), F32),
                    pltpu.VMEM((STEPS, 8, block), F32),
                ]
            else:
                outs += [shape((8, length), F32)]
                for k in sorted(stages[n + 1] if n == 0 else [j for j in stages[n + 1] if not j & (j - 1)]):
                    if partial:
                        partial[2], even[k] = lax.optimization_barrier((partial[2], even[k]))
                    else:
                        moved_rest, even[k] = lax.optimization_barrier((moved_rest, even[k]))
                    odd.append(swap(even[k], "dom", dom, 1))
            if n > 1:
                for k in stage:
                    if k & (k - 1):
                        partial[2], even[k] = lax.optimization_barrier((partial[2], even[k]))
                        odd.append(swap(even[k], "dom", dom, 1))
            results = call(
                lambda *r: body(
                    *r,
                    count=count,
                    others=len(rest),
                    length=length,
                    rest_at=2 * stage[0] * width,
                    **options,
                ),
                outs + [held] * pairs,
                "score",
                scratch,
                limit=6 if last else 6,
                aliases=aliases,
            )(
                *[m for k in stage for m in (even[k], odd[k])],
                *[moved[k] for k in stage],
                moved_rest,
                *partial,
                *[moved[k] for k in rest],
            )
            partial, moved = list(results[:first_held]), results[first_held:]
        weights, weights_rest, tops, stats = partial

        gathered = [stats] + [swap(stats, "cls", cls, k) for k in range(1, cls)]

        accumulator = pltpu.VMEM((h, 2 * width), F32)
        order = sorted(range(1, pairs), key=lambda k: (k & -k, -k)) + [0]
        sent = {}

        def children(k):
            low = k & -k or pairs
            return [sent[k | 1 << t] for t in range(low.bit_length() - 1)]

        probs, probs_rest, own, other, weight_row, *kept = call(
            lambda *r: first_sums_body(
                *r, groups=cls, others=pairs - 1, length=length, rest_at=order[0] * 2 * width
            ),
            [
                shape((STEPS, h, block), BF16),
                shape((h, rows), BF16),
                shape((h, width), F32),
                shape((h + TAIL, width), BF16),
                shape((8, length), F32),
            ]
            + [held] * (pairs - 1),
            "sums_first",
            aliases={cls + 5 + k: 5 + k for k in range(pairs - 1)},
            limit=2,
            scratch=[
                accumulator,
                pltpu.VMEM((8, block), F32),
                pltpu.VMEM((8, block), F32),
                pltpu.VMEM(tops.shape, F32),
                pltpu.VMEM((h, 128), F32),
                pltpu.VMEM((length, 128), F32),
                pltpu.VMEM((TAIL, width), F32),
            ],
        )(
            *gathered,
            weights,
            weights_rest,
            tops,
            moved[order[0]],
            moved_rest,
            *[moved[k] for k in order[1:]],
        )
        received = swap(other, "dom", dom, 1)
        first, chip_row = call(
            first_pair_body,
            [shape((h + TAIL, width), BF16), shape((8, length), F32)],
            "pair_first",
            [pltpu.VMEM((TAIL, width), F32)],
        )(own, received, weight_row)
        sent[order[0]] = swap(first, "dom", dom, 2 * (order[0] & -order[0]))
        ready = first

        for n, k in enumerate(order[1:]):
            if n:
                probs_rest, ready = lax.optimization_barrier((probs_rest, ready))
            others = pairs - 2 - n
            own, other, *kept = call(
                lambda *r: sums_body(*r, others=others, rest_at=k * 2 * width),
                [shape((h, width), F32), shape((h, width), BF16)] + [held] * others,
                "sums",
                [accumulator],
                aliases={4 + j: 2 + j for j in range(others)},
            )(probs, probs_rest, kept[0], moved_rest, *kept[1:])
            received = swap(other, "dom", dom, 1)
            if k:
                (ready,) = call(
                    pair_body,
                    [shape((h + TAIL, width), BF16)],
                    "pair",
                    [pltpu.VMEM((TAIL, width), F32)],
                )(own, received, chip_row, *children(k))
                sent[k] = swap(ready, "dom", dom, 2 * (k & -k))

        arrived = children(0)
        sums, class_weight = call(
            lambda *r: finish_body(*r, count=len(arrived)),
            [shape((h, width), F32), shape((classes, rotations), F32)],
            "finish",
        )(*arrived, own, received, chip_row)
        return sums.reshape(rotations, classes, width).transpose(1, 0, 2), class_weight

    return on_device


def solution(mesh):
    return jax.shard_map(
        make_on_device(mesh.shape["dom"], mesh.shape["cls"]),
        mesh=mesh,
        in_specs=(P("dom", "cls"), P("cls", None, "dom"), P()),
        out_specs=(P("cls", None, "dom"), P("cls", None)),
        check_vma=False,
    )
```

```python
import math

import jax
import jax.numpy as jnp
import numpy as np
from jax import lax
from jax.experimental import pallas as pl
from jax.experimental.pallas import tpu as pltpu
from jax.sharding import PartitionSpec as P

WIN = 32
BOX = 64
SHIFT_SIDE = 9
SHIFTS = SHIFT_SIDE * SHIFT_SIDE
HALF = WIN * WIN
F = 2 * HALF
GROUP = 8
MAIN = SHIFTS // GROUP * GROUP
STEPS = MAIN // GROUP
TAIL = 8
F32 = jnp.float32
BF16 = jnp.bfloat16


def phase_tables():
    freq = np.arange(HALF)
    fy = freq // WIN - WIN // 2
    fx = freq % WIN - WIN // 2
    offset = np.arange(MAIN // 2)
    sy = offset // SHIFT_SIDE - SHIFT_SIDE // 2
    sx = offset % SHIFT_SIDE - SHIFT_SIDE // 2
    turns = sx[:, None] * fx[None, :] + sy[:, None] * fy[None, :]
    theta = (2.0 * math.pi / BOX) * turns
    return np.stack([np.cos(theta), np.sin(theta)]).astype(np.float32)


def contract(x, y, dims):
    return lax.dot_general(x, y, (dims, ((), ())), preferred_element_type=F32)


def spread(row):
    high = row.astype(BF16).astype(F32)
    rest = row - high
    mid = rest.astype(BF16).astype(F32)
    low = (rest - mid).astype(BF16).astype(F32)
    return high, mid, low


def column_to_row(column, length, scratch):
    h = column.shape[0]
    scratch[...] = jnp.zeros(scratch.shape, F32)
    scratch[0:h, :] = jnp.broadcast_to(column, (h, 128))
    return scratch[...].T[0:1, :]


def tail_block(row, width, scratch):
    scratch[...] = jnp.zeros(scratch.shape, F32)
    per = row.shape[1] // width
    for p, part in enumerate(spread(row)):
        for j in range(per):
            r = p * per + j
            scratch[r : r + 1, :] = part[:, j * width : (j + 1) * width]
    return scratch[...].astype(BF16)


def row_of_tail(tail, width, length):
    per = length // width
    pieces = []
    for j in range(per):
        rows = [tail[p * per + j : p * per + j + 1, :] for p in range(3)]
        pieces.append((rows[2] + rows[1]) + rows[0])
    return jnp.concatenate(pieces, axis=1) if per > 1 else pieces[0]


def begin_body(*refs, width):
    place = lax.axis_index("dom")
    sources = refs[:4]
    message, cosine, sine, kept, x_ref, noise, tables, tall, tail, arrived = refs[4:]
    copies = [
        pltpu.make_async_copy(source, target, arrived.at[n])
        for n, (source, target) in enumerate(zip(sources, (x_ref, noise, tables, kept)))
    ]
    for copy in copies:
        copy.start()
    count = HALF // width
    at = pl.multiple_of(jnp.bitwise_and(place, count - 1) * width, 128)
    h = x_ref.shape[0]
    copies[0].wait()
    copies[1].wait()
    x = x_ref[...]
    w = noise[:, pl.ds(at, width)]
    message[0:h, :] = (x * w).astype(BF16)
    half = 0.5 * jnp.sum(x * x * w, axis=1, keepdims=True)
    row = column_to_row(half, tall.shape[0], tall)
    message[h : h + TAIL, :] = tail_block(row, width, tail)
    copies[2].wait()
    sign = jnp.where(place < count, 1.0, -1.0).astype(F32)
    for k in range(count):
        at = pl.multiple_of(jnp.bitwise_and(jnp.bitwise_xor(place, k), count - 1) * width, 128)
        cosine[:, k * width : (k + 1) * width] = tables[0, :, pl.ds(at, width)]
        sine[:, k * width : (k + 1) * width] = tables[1, :, pl.ds(at, width)] * sign
    copies[3].wait()


def shift_body(*refs, parts, pairs, width):
    pieces = refs[:parts]
    cosine, sine = refs[parts : parts + 2]
    outs = refs[parts + 2 : parts + 2 + pairs]
    rest, plain, whole = refs[parts + 2 + pairs :]
    rows, part_width = pieces[0].shape
    place = lax.axis_index("dom")
    column = lax.axis_index("cls")
    for k in range(parts):
        at = pl.multiple_of(jnp.bitwise_xor(column, k) * part_width, 128)
        plain[:, pl.ds(at, part_width)] = pieces[k][...].astype(F32)
    for k in range(2 * pairs):
        at = pl.multiple_of(jnp.bitwise_xor(place, k) * width, 128)
        whole[:, k * width : (k + 1) * width] = plain[:, pl.ds(at, width)]
    rest[...] = whole[...].astype(BF16)

    def one(s, carry):
        at = pl.multiple_of(2 * s * rows, rows)
        back = pl.multiple_of((2 * s + 1) * rows, rows)
        c_all = cosine[pl.ds(s, 1), :]
        s_all = sine[pl.ds(s, 1), :]
        for k in range(pairs):
            q = k * width
            c_row = c_all[:, q : q + width]
            s_row = s_all[:, q : q + width]
            a = whole[:, q : q + width]
            b = whole[:, HALF + q : HALF + q + width]
            ac, bs, bc, sa = a * c_row, b * s_row, b * c_row, a * s_row
            low = slice((k % 2) * width, (k % 2 + 1) * width)
            outs[k // 2][pl.ds(at, rows), low] = (ac + bs).astype(BF16)
            outs[(k + pairs) // 2][pl.ds(at, rows), low] = (bc - sa).astype(BF16)
            outs[k // 2][pl.ds(back, rows), low] = (ac - bs).astype(BF16)
            outs[(k + pairs) // 2][pl.ds(back, rows), low] = (bc + sa).astype(BF16)
        return carry

    lax.fori_loop(0, MAIN // 2, one, 0)


def load_slabs(slabs, weighted, row, length):
    h = weighted.shape[0]
    width = slabs[0].shape[1]
    for k, slab in enumerate(slabs):
        weighted[:, k * width : (k + 1) * width] = slab[0:h, :]
        row += row_of_tail(slab[h : h + TAIL, :].astype(F32), width, length)
    return row


def stage_body(*refs, first, count, others, length, rest_at):
    slabs, moved, moved_rest = refs[: 2 * count], refs[2 * count : 3 * count], refs[3 * count]
    at = 3 * count + 1
    partial = None if first else refs[at : at + 3]
    at += (0 if first else 3) + others
    scores, scores_rest, norms = refs[at : at + 3]
    weighted = refs[-1]
    span = weighted.shape[1]
    block = scores.shape[2]
    row = jnp.zeros((1, length), F32) if first else partial[2][0:1, :]
    norms[...] = jnp.broadcast_to(load_slabs(slabs, weighted, row, length), norms.shape)
    last = contract(weighted[...], moved_rest[:, rest_at : rest_at + span], ((1,), (1,)))
    scores_rest[...] = last if first else partial[1][...] + last
    for i in range(STEPS):
        x = jnp.concatenate([m[i * block : (i + 1) * block, :] for m in moved], axis=1)
        x = contract(weighted[...], x, ((1,), (1,)))
        scores[i] = x if first else partial[0][i] + x


def last_stage_body(*refs, count, others, length, rest_at):
    slabs, moved, moved_rest = refs[: 2 * count], refs[2 * count : 3 * count], refs[3 * count]
    scores, scores_rest, norms = refs[3 * count + 1 : 3 * count + 4]
    at = 3 * count + 4 + others
    weights, weights_rest, tops, stats = refs[at : at + 4]
    weighted, half, even, odd, totals = refs[-5:]
    h, block = even.shape
    rows = moved_rest.shape[0]
    span = weighted.shape[1]
    row = load_slabs(slabs, weighted, norms[0:1, :], length)
    half[...] = jnp.broadcast_to(row, (128, length)).T[0:h, :]

    def multiply(i, target):
        x = jnp.concatenate([m[i * block : (i + 1) * block, :] for m in moved], axis=1)
        target[...] = scores[i] + contract(weighted[...], x, ((1,), (1,)))

    def soften(i, source):
        for q in range(0, block, 128):
            x = source[:, q : q + 128] - half[...]
            top = jnp.max(x, axis=0, keepdims=True)
            x = jnp.exp(x - top)
            weights[i, :, q : q + 128] = x
            tops[i, :, q : q + 128] = jnp.broadcast_to(top, (8, 128))
            total = jnp.sum(x, axis=0, keepdims=True)
            totals[i, :, q : q + 128] = jnp.broadcast_to(total, (8, 128))

    multiply(0, even)
    for i in range(1, STEPS):
        multiply(i, odd if i % 2 else even)
        soften(i - 1, even if i % 2 else odd)
    last = contract(weighted[...], moved_rest[:, rest_at : rest_at + span], ((1,), (1,)))
    last = scores_rest[...] + last - half[:, 0:1]
    soften(STEPS - 1, odd if (STEPS - 1) % 2 else even)

    best = jnp.max(last, axis=0, keepdims=True)
    last = jnp.exp(last - best)
    weights_rest[...] = last
    tops[STEPS, 0:1, 0:rows] = best
    mass = jnp.sum(last, axis=0, keepdims=True)
    lane_top = tops[0]
    for i in range(1, STEPS):
        lane_top = jnp.maximum(lane_top, tops[i])
    lane_mass = totals[0] * jnp.exp(tops[0] - lane_top)
    for i in range(1, STEPS):
        lane_mass += totals[i] * jnp.exp(tops[i] - lane_top)
    parts_top = [lane_top[0:1, j * rows : (j + 1) * rows] for j in range(GROUP)]
    peak = best
    for t in parts_top:
        peak = jnp.maximum(peak, t)
    mass = mass * jnp.exp(best - peak)
    for j in range(GROUP):
        mass += lane_mass[0:1, j * rows : (j + 1) * rows] * jnp.exp(parts_top[j] - peak)
    stats[...] = jnp.zeros(stats.shape, F32)
    stats[0:1, 0:rows] = peak
    stats[1:2, 0:rows] = mass


def split_pair(sums, own, other):
    h, width = own.shape
    own[...] = sums[:, 0:width]
    other[0:h, :] = sums[:, width : 2 * width].astype(BF16)


def accumulate(sums, probs, probs_rest, moved, moved_rest, rest_at, ahead=None):
    block = probs.shape[2]
    if ahead:
        ahead(0)
    sums[...] = contract(probs_rest[...], moved_rest[:, rest_at : rest_at + sums.shape[1]], ((1,), (0,)))
    for i in range(STEPS):
        sums[...] += contract(probs[i], moved[i * block : (i + 1) * block, :], ((1,), (0,)))
        if ahead and i + 1 < STEPS:
            ahead(i + 1)


def first_sums_body(*refs, groups, others, length, rest_at):
    gathered = refs[:groups]
    weights, weights_rest, tops, moved, moved_rest = refs[groups : groups + 5]
    probs, probs_rest, own, other, weight_row = refs[groups + 5 + others : groups + 10 + others]
    sums, peak, inverse, scale, mass, tall, tail = refs[-7:]
    h, width = own.shape
    rows = moved_rest.shape[0]
    block = probs.shape[2]

    best = gathered[0][0:1, 0:rows]
    for g in gathered[1:]:
        best = jnp.maximum(best, g[0:1, 0:rows])
    whole = jnp.zeros((1, rows), F32)
    for g in gathered:
        whole += g[1:2, 0:rows] * jnp.exp(g[0:1, 0:rows] - best)
    over = 1.0 / whole
    for j in range(GROUP):
        peak[:, j * rows : (j + 1) * rows] = jnp.broadcast_to(best, (8, rows))
        inverse[:, j * rows : (j + 1) * rows] = jnp.broadcast_to(over, (8, rows))
    for i in range(STEPS):
        scale[i] = jnp.exp(tops[i] - peak[...]) * inverse[...]

    last = weights_rest[...] * (jnp.exp(tops[STEPS, 0:1, 0:rows] - best) * over)
    last_low = last.astype(BF16)
    probs_rest[...] = last_low
    mass[...] = jnp.zeros(mass.shape, F32)
    mass[:, 0:1] = jnp.sum(last, axis=1, keepdims=True)

    def normalise(i):
        part = mass[...]
        for q in range(0, block, 128):
            prob = weights[i, :, q : q + 128] * scale[i, 0:1, q : q + 128]
            probs[i, :, q : q + 128] = prob.astype(BF16)
            part += prob
        mass[...] = part

    accumulate(sums, probs, probs_rest, moved, moved_rest, rest_at, normalise)
    split_pair(sums, own, other)
    row = column_to_row(jnp.sum(mass[...], axis=1, keepdims=True), length, tall)
    weight_row[...] = jnp.broadcast_to(row, weight_row.shape)
    other[h : h + TAIL, :] = tail_block(row, width, tail)


def sums_body(probs, probs_rest, moved, moved_rest, *refs, others, rest_at):
    own, other = refs[others : others + 2]
    sums = refs[-1]
    accumulate(sums, probs, probs_rest, moved, moved_rest, rest_at)
    split_pair(sums, own, other)


def first_pair_body(own, received, weight_row, message, chip_row, tail):
    h, width = own.shape
    message[0:h, :] = (own[...] + received[0:h, :].astype(F32)).astype(BF16)
    length = weight_row.shape[1]
    row = weight_row[0:1, :] + row_of_tail(received[h : h + TAIL, :].astype(F32), width, length)
    chip_row[...] = jnp.broadcast_to(row, chip_row.shape)
    message[h : h + TAIL, :] = tail_block(row, width, tail)


def pair_body(own, received, chip_row, *refs):
    arrived = refs[:-2]
    message, tail = refs[-2:]
    h, width = own.shape
    length = chip_row.shape[1]
    x = own[...] + received[...].astype(F32)
    row = chip_row[0:1, :]
    for m in arrived:
        x += m[0:h, :].astype(F32)
        row += row_of_tail(m[h : h + TAIL, :].astype(F32), width, length)
    message[0:h, :] = x.astype(BF16)
    message[h : h + TAIL, :] = tail_block(row, width, tail)


def finish_body(*refs, count):
    messages = refs[:count]
    own, received, chip_row, class_sums, class_weight = refs[count:]
    h, width = own.shape
    rotations, classes = class_weight.shape[1], class_weight.shape[0]
    length = chip_row.shape[1]
    x = own[...] + received[...].astype(F32)
    row = chip_row[0:1, :]
    for m in messages:
        x += m[0:h, :].astype(F32)
        row += row_of_tail(m[h : h + TAIL, :].astype(F32), width, length)
    class_sums[...] = x
    shape = (classes, length)
    at = lax.broadcasted_iota(jnp.int32, shape, 1)
    mine = at - at // classes * classes == lax.broadcasted_iota(jnp.int32, shape, 0)
    spread_out = jnp.where(mine, jnp.broadcast_to(row, shape), 0.0)
    shape = (length, rotations)
    pick = lax.broadcasted_iota(jnp.int32, shape, 0) // classes == lax.broadcasted_iota(
        jnp.int32, shape, 1
    )
    class_weight[...] = lax.dot_general(
        spread_out,
        pick.astype(F32),
        (((1,), (0,)), ((), ())),
        precision=lax.Precision.HIGHEST,
        preferred_element_type=F32,
    )


VMEM = pl.BlockSpec(memory_space=pltpu.VMEM)


def make_on_device(dom, cls):
    pairs = dom // 2

    def swap(x, axis, size, k):
        return lax.ppermute(x, axis, [(i, i ^ k) for i in range(size)])

    def on_device(particles, references, noise_weight):
        rows, part_width = particles.shape
        classes, rotations, width = references.shape
        h = classes * rotations
        length = -(-h // width) * width
        block = GROUP * rows
        shape = jax.ShapeDtypeStruct

        def call(body, shapes, name, scratch=(), limit=2, aliases=None, inputs=VMEM, flops=1):
            def run(*args):
                specs = [inputs] * len(args)
                spec = pltpu.PrefetchScalarGridSpec(
                    num_scalar_prefetch=0,
                    grid=(),
                    in_specs=specs,
                    out_specs=[VMEM] * len(shapes),
                    scratch_shapes=list(scratch),
                )
                params = pltpu.CompilerParams(vmem_limit_bytes=limit * 1024 * 1024)
                return pl.pallas_call(
                    body,
                    grid_spec=spec,
                    out_shape=shapes,
                    compiler_params=params,
                    input_output_aliases=aliases or {},
                    cost_estimate=pl.CostEstimate(flops=flops, transcendentals=0, bytes_accessed=1),
                    name=name,
                )(*args)

            return run

        pieces = [particles] + [swap(particles, "cls", cls, k) for k in range(1, cls)]

        tables = phase_tables()
        ref_rows = references.transpose(1, 0, 2).reshape(h, width)
        message, *angles, pieces[0] = call(
            lambda *r: begin_body(*r, width=width),
            [shape((h + TAIL, width), BF16)]
            + [shape(tables.shape[1:], F32)] * 2
            + [shape(particles.shape, BF16)],
            "begin",
            [
                pltpu.VMEM((h, width), F32),
                pltpu.VMEM((1, HALF), F32),
                pltpu.VMEM(tables.shape, F32),
                pltpu.VMEM((length, 128), F32),
                pltpu.VMEM((TAIL, width), F32),
                pltpu.SemaphoreType.DMA((4,)),
            ],
            inputs=pl.BlockSpec(memory_space=pltpu.HBM),
        )(
            *[
                pltpu.with_memory_space_constraint(x, pltpu.HBM)
                for x in (ref_rows, noise_weight.reshape(1, HALF), jnp.asarray(tables), particles)
            ],
        )

        even = [message] + [None] * (pairs - 1)
        for k in range(1, pairs):
            if not k & (k - 1):
                even[k] = swap(message, "dom", dom, 2 * k)
        odd = [swap(message, "dom", dom, 1)]

        *moved, moved_rest = call(
            lambda *r: shift_body(*r, parts=cls, pairs=pairs, width=width),
            [pltpu.VMEM((MAIN * rows, 2 * width), BF16)] * pairs + [shape((rows, F), BF16)],
            "shift",
            flops=10**10,
            limit=2,
            scratch=[pltpu.VMEM((rows, F), F32)] * 2,
        )(*pieces, *angles)

        for k in range(1, pairs):
            if k & (k - 1):
                source = k & (k - 1)
                moved_rest, even[source] = lax.optimization_barrier((moved_rest, even[source]))
                even[k] = swap(even[source], "dom", dom, 2 * (k & -k))

        held = pltpu.VMEM((MAIN * rows, 2 * width), BF16)
        partial = []
        stages = [[0]] + [list(range(1 << t, 2 << t)) for t in range((pairs - 1).bit_length())]
        for n, stage in enumerate(stages):
            last = stage[-1] == pairs - 1
            count = len(stage)
            rest = [k for k in range(pairs) if k not in stage]
            first_held = 4 if last else 3
            after = 3 * count + 1 + len(partial)
            aliases = {2 * count + m: first_held + k for m, k in enumerate(stage)}
            aliases |= {after + m: first_held + k for m, k in enumerate(rest)}
            if partial:
                aliases |= {3 * count + 1: 0, 3 * count + 2: 1}
            body = last_stage_body if last else stage_body
            options = {} if last else {"first": not partial}
            outs = [pltpu.VMEM((STEPS, h, block), F32), shape((h, rows), F32)]
            scratch = [pltpu.VMEM((h, 2 * width * count), BF16)]
            if last:
                outs += [shape((STEPS + 1, 8, block), F32), shape((8, 128), F32)]
                scratch += [
                    pltpu.VMEM((h, 128), F32),
                    pltpu.VMEM((h, block), F32),
                    pltpu.VMEM((h, block), F32),
                    pltpu.VMEM((STEPS, 8, block), F32),
                ]
            else:
                outs += [shape((8, length), F32)]
                for k in sorted(stages[n + 1] if n == 0 else [j for j in stages[n + 1] if not j & (j - 1)]):
                    if partial:
                        partial[2], even[k] = lax.optimization_barrier((partial[2], even[k]))
                    else:
                        moved_rest, even[k] = lax.optimization_barrier((moved_rest, even[k]))
                    odd.append(swap(even[k], "dom", dom, 1))
            if n > 1:
                for k in stage:
                    if k & (k - 1):
                        partial[2], even[k] = lax.optimization_barrier((partial[2], even[k]))
                        odd.append(swap(even[k], "dom", dom, 1))
            results = call(
                lambda *r: body(
                    *r,
                    count=count,
                    others=len(rest),
                    length=length,
                    rest_at=2 * stage[0] * width,
                    **options,
                ),
                outs + [held] * pairs,
                "score",
                scratch,
                limit=6 if last else 6,
                aliases=aliases,
            )(
                *[m for k in stage for m in (even[k], odd[k])],
                *[moved[k] for k in stage],
                moved_rest,
                *partial,
                *[moved[k] for k in rest],
            )
            partial, moved = list(results[:first_held]), results[first_held:]
        weights, weights_rest, tops, stats = partial

        gathered = [stats] + [swap(stats, "cls", cls, k) for k in range(1, cls)]

        accumulator = pltpu.VMEM((h, 2 * width), F32)
        order = sorted(range(1, pairs), key=lambda k: (k & -k, -k)) + [0]
        sent = {}

        def children(k):
            low = k & -k or pairs
            return [sent[k | 1 << t] for t in range(low.bit_length() - 1)]

        probs, probs_rest, own, other, weight_row, *kept = call(
            lambda *r: first_sums_body(
                *r, groups=cls, others=pairs - 1, length=length, rest_at=order[0] * 2 * width
            ),
            [
                shape((STEPS, h, block), BF16),
                shape((h, rows), BF16),
                shape((h, width), F32),
                shape((h + TAIL, width), BF16),
                shape((8, length), F32),
            ]
            + [held] * (pairs - 1),
            "sums_first",
            aliases={cls + 5 + k: 5 + k for k in range(pairs - 1)},
            limit=2,
            scratch=[
                accumulator,
                pltpu.VMEM((8, block), F32),
                pltpu.VMEM((8, block), F32),
                pltpu.VMEM(tops.shape, F32),
                pltpu.VMEM((h, 128), F32),
                pltpu.VMEM((length, 128), F32),
                pltpu.VMEM((TAIL, width), F32),
            ],
        )(
            *gathered,
            weights,
            weights_rest,
            tops,
            moved[order[0]],
            moved_rest,
            *[moved[k] for k in order[1:]],
        )
        received = swap(other, "dom", dom, 1)
        first, chip_row = call(
            first_pair_body,
            [shape((h + TAIL, width), BF16), shape((8, length), F32)],
            "pair_first",
            [pltpu.VMEM((TAIL, width), F32)],
        )(own, received, weight_row)
        sent[order[0]] = swap(first, "dom", dom, 2 * (order[0] & -order[0]))
        ready = first

        for n, k in enumerate(order[1:]):
            if n:
                probs_rest, ready = lax.optimization_barrier((probs_rest, ready))
            others = pairs - 2 - n
            own, other, *kept = call(
                lambda *r: sums_body(*r, others=others, rest_at=k * 2 * width),
                [shape((h, width), F32), shape((h, width), BF16)] + [held] * others,
                "sums",
                [accumulator],
                aliases={4 + j: 2 + j for j in range(others)},
            )(probs, probs_rest, kept[0], moved_rest, *kept[1:])
            received = swap(other, "dom", dom, 1)
            if k:
                (ready,) = call(
                    pair_body,
                    [shape((h + TAIL, width), BF16)],
                    "pair",
                    [pltpu.VMEM((TAIL, width), F32)],
                )(own, received, chip_row, *children(k))
                sent[k] = swap(ready, "dom", dom, 2 * (k & -k))

        arrived = children(0)
        sums, class_weight = call(
            lambda *r: finish_body(*r, count=len(arrived)),
            [shape((h, width), F32), shape((classes, rotations), F32)],
            "finish",
        )(*arrived, own, received, chip_row)
        return sums.reshape(rotations, classes, width).transpose(1, 0, 2), class_weight

    return on_device


def solution(mesh):
    return jax.shard_map(
        make_on_device(mesh.shape["dom"], mesh.shape["cls"]),
        mesh=mesh,
        in_specs=(P("dom", "cls"), P("cls", None, "dom"), P()),
        out_specs=(P("cls", None, "dom"), P("cls", None)),
        check_vma=False,
    )
```

```python
import math

import jax
import jax.numpy as jnp
import numpy as np
from jax import lax
from jax.experimental import pallas as pl
from jax.experimental.pallas import tpu as pltpu
from jax.sharding import PartitionSpec as P

WIN = 32
BOX = 64
SHIFT_SIDE = 9
SHIFTS = SHIFT_SIDE * SHIFT_SIDE
HALF = WIN * WIN
F = 2 * HALF
GROUP = 8
MAIN = SHIFTS // GROUP * GROUP
STEPS = MAIN // GROUP
TAIL = 8
F32 = jnp.float32
BF16 = jnp.bfloat16


def phase_tables():
    freq = np.arange(HALF)
    fy = freq // WIN - WIN // 2
    fx = freq % WIN - WIN // 2
    offset = np.arange(MAIN // 2)
    sy = offset // SHIFT_SIDE - SHIFT_SIDE // 2
    sx = offset % SHIFT_SIDE - SHIFT_SIDE // 2
    turns = sx[:, None] * fx[None, :] + sy[:, None] * fy[None, :]
    theta = (2.0 * math.pi / BOX) * turns
    return np.stack([np.cos(theta), np.sin(theta)]).astype(np.float32)


def contract(x, y, dims):
    return lax.dot_general(x, y, (dims, ((), ())), preferred_element_type=F32)


def spread(row):
    high = row.astype(BF16).astype(F32)
    rest = row - high
    mid = rest.astype(BF16).astype(F32)
    low = (rest - mid).astype(BF16).astype(F32)
    return high, mid, low


def column_to_row(column, length, scratch):
    h = column.shape[0]
    scratch[...] = jnp.zeros(scratch.shape, F32)
    scratch[0:h, :] = jnp.broadcast_to(column, (h, 128))
    return scratch[...].T[0:1, :]


def tail_block(row, width, scratch):
    scratch[...] = jnp.zeros(scratch.shape, F32)
    per = row.shape[1] // width
    for p, part in enumerate(spread(row)):
        for j in range(per):
            r = p * per + j
            scratch[r : r + 1, :] = part[:, j * width : (j + 1) * width]
    return scratch[...].astype(BF16)


def row_of_tail(tail, width, length):
    per = length // width
    pieces = []
    for j in range(per):
        rows = [tail[p * per + j : p * per + j + 1, :] for p in range(3)]
        pieces.append((rows[2] + rows[1]) + rows[0])
    return jnp.concatenate(pieces, axis=1) if per > 1 else pieces[0]


def begin_body(*refs, width):
    place = lax.axis_index("dom")
    sources = refs[:4]
    message, cosine, sine, kept, x_ref, noise, tables, tall, tail, arrived = refs[4:]
    copies = [
        pltpu.make_async_copy(source, target, arrived.at[n])
        for n, (source, target) in enumerate(zip(sources, (x_ref, noise, tables, kept)))
    ]
    for copy in copies:
        copy.start()
    count = HALF // width
    at = pl.multiple_of(jnp.bitwise_and(place, count - 1) * width, 128)
    h = x_ref.shape[0]
    copies[0].wait()
    copies[1].wait()
    x = x_ref[...]
    w = noise[:, pl.ds(at, width)]
    message[0:h, :] = (x * w).astype(BF16)
    half = 0.5 * jnp.sum(x * x * w, axis=1, keepdims=True)
    row = column_to_row(half, tall.shape[0], tall)
    message[h : h + TAIL, :] = tail_block(row, width, tail)
    copies[2].wait()
    sign = jnp.where(place < count, 1.0, -1.0).astype(F32)
    for k in range(count):
        at = pl.multiple_of(jnp.bitwise_and(jnp.bitwise_xor(place, k), count - 1) * width, 128)
        cosine[:, k * width : (k + 1) * width] = tables[0, :, pl.ds(at, width)]
        sine[:, k * width : (k + 1) * width] = tables[1, :, pl.ds(at, width)] * sign
    copies[3].wait()


def shift_body(*refs, parts, pairs, width):
    pieces = refs[:parts]
    cosine, sine = refs[parts : parts + 2]
    outs = refs[parts + 2 : parts + 2 + pairs]
    rest, plain, whole = refs[parts + 2 + pairs :]
    rows, part_width = pieces[0].shape
    place = lax.axis_index("dom")
    column = lax.axis_index("cls")
    for k in range(parts):
        at = pl.multiple_of(jnp.bitwise_xor(column, k) * part_width, 128)
        plain[:, pl.ds(at, part_width)] = pieces[k][...].astype(F32)
    for k in range(2 * pairs):
        at = pl.multiple_of(jnp.bitwise_xor(place, k) * width, 128)
        whole[:, k * width : (k + 1) * width] = plain[:, pl.ds(at, width)]
    rest[...] = whole[...].astype(BF16)

    def one(s, carry):
        at = pl.multiple_of(2 * s * rows, rows)
        back = pl.multiple_of((2 * s + 1) * rows, rows)
        c_all = cosine[pl.ds(s, 1), :]
        s_all = sine[pl.ds(s, 1), :]
        for k in range(pairs):
            q = k * width
            c_row = c_all[:, q : q + width]
            s_row = s_all[:, q : q + width]
            a = whole[:, q : q + width]
            b = whole[:, HALF + q : HALF + q + width]
            ac, bs, bc, sa = a * c_row, b * s_row, b * c_row, a * s_row
            low = slice((k % 2) * width, (k % 2 + 1) * width)
            outs[k // 2][pl.ds(at, rows), low] = (ac + bs).astype(BF16)
            outs[(k + pairs) // 2][pl.ds(at, rows), low] = (bc - sa).astype(BF16)
            outs[k // 2][pl.ds(back, rows), low] = (ac - bs).astype(BF16)
            outs[(k + pairs) // 2][pl.ds(back, rows), low] = (bc + sa).astype(BF16)
        return carry

    lax.fori_loop(0, MAIN // 2, one, 0)


def load_slabs(slabs, weighted, row, length):
    h = weighted.shape[0]
    width = slabs[0].shape[1]
    for k, slab in enumerate(slabs):
        weighted[:, k * width : (k + 1) * width] = slab[0:h, :]
        row += row_of_tail(slab[h : h + TAIL, :].astype(F32), width, length)
    return row


def stage_body(*refs, first, count, others, length, rest_at):
    slabs, moved, moved_rest = refs[: 2 * count], refs[2 * count : 3 * count], refs[3 * count]
    at = 3 * count + 1
    partial = None if first else refs[at : at + 3]
    at += (0 if first else 3) + others
    scores, scores_rest, norms = refs[at : at + 3]
    weighted = refs[-1]
    span = weighted.shape[1]
    block = scores.shape[2]
    row = jnp.zeros((1, length), F32) if first else partial[2][0:1, :]
    norms[...] = jnp.broadcast_to(load_slabs(slabs, weighted, row, length), norms.shape)
    last = contract(weighted[...], moved_rest[:, rest_at : rest_at + span], ((1,), (1,)))
    scores_rest[...] = last if first else partial[1][...] + last
    for i in range(STEPS):
        x = jnp.concatenate([m[i * block : (i + 1) * block, :] for m in moved], axis=1)
        x = contract(weighted[...], x, ((1,), (1,)))
        scores[i] = x if first else partial[0][i] + x


def last_stage_body(*refs, count, others, length, rest_at):
    slabs, moved, moved_rest = refs[: 2 * count], refs[2 * count : 3 * count], refs[3 * count]
    scores, scores_rest, norms = refs[3 * count + 1 : 3 * count + 4]
    at = 3 * count + 4 + others
    weights, weights_rest, tops, stats = refs[at : at + 4]
    weighted, half, even, odd, totals = refs[-5:]
    h, block = even.shape
    rows = moved_rest.shape[0]
    span = weighted.shape[1]
    row = load_slabs(slabs, weighted, norms[0:1, :], length)
    half[...] = jnp.broadcast_to(row, (128, length)).T[0:h, :]

    def multiply(i, target):
        x = jnp.concatenate([m[i * block : (i + 1) * block, :] for m in moved], axis=1)
        target[...] = scores[i] + contract(weighted[...], x, ((1,), (1,)))

    def soften(i, source):
        for q in range(0, block, 128):
            x = source[:, q : q + 128] - half[...]
            top = jnp.max(x, axis=0, keepdims=True)
            x = jnp.exp(x - top)
            weights[i, :, q : q + 128] = x
            tops[i, :, q : q + 128] = jnp.broadcast_to(top, (8, 128))
            total = jnp.sum(x, axis=0, keepdims=True)
            totals[i, :, q : q + 128] = jnp.broadcast_to(total, (8, 128))

    multiply(0, even)
    for i in range(1, STEPS):
        multiply(i, odd if i % 2 else even)
        soften(i - 1, even if i % 2 else odd)
    last = contract(weighted[...], moved_rest[:, rest_at : rest_at + span], ((1,), (1,)))
    last = scores_rest[...] + last - half[:, 0:1]
    soften(STEPS - 1, odd if (STEPS - 1) % 2 else even)

    best = jnp.max(last, axis=0, keepdims=True)
    last = jnp.exp(last - best)
    weights_rest[...] = last
    tops[STEPS, 0:1, 0:rows] = best
    mass = jnp.sum(last, axis=0, keepdims=True)
    lane_top = tops[0]
    for i in range(1, STEPS):
        lane_top = jnp.maximum(lane_top, tops[i])
    lane_mass = totals[0] * jnp.exp(tops[0] - lane_top)
    for i in range(1, STEPS):
        lane_mass += totals[i] * jnp.exp(tops[i] - lane_top)
    parts_top = [lane_top[0:1, j * rows : (j + 1) * rows] for j in range(GROUP)]
    peak = best
    for t in parts_top:
        peak = jnp.maximum(peak, t)
    mass = mass * jnp.exp(best - peak)
    for j in range(GROUP):
        mass += lane_mass[0:1, j * rows : (j + 1) * rows] * jnp.exp(parts_top[j] - peak)
    stats[...] = jnp.zeros(stats.shape, F32)
    stats[0:1, 0:rows] = peak
    stats[1:2, 0:rows] = mass


def split_pair(sums, own, other):
    h, width = own.shape
    own[...] = sums[:, 0:width]
    other[0:h, :] = sums[:, width : 2 * width].astype(BF16)


def accumulate(sums, probs, probs_rest, moved, moved_rest, rest_at, ahead=None):
    block = probs.shape[2]
    if ahead:
        ahead(0)
    sums[...] = contract(probs_rest[...], moved_rest[:, rest_at : rest_at + sums.shape[1]], ((1,), (0,)))
    for i in range(STEPS):
        sums[...] += contract(probs[i], moved[i * block : (i + 1) * block, :], ((1,), (0,)))
        if ahead and i + 1 < STEPS:
            ahead(i + 1)


def first_sums_body(*refs, groups, others, length, rest_at):
    gathered = refs[:groups]
    weights, weights_rest, tops, moved, moved_rest = refs[groups : groups + 5]
    probs, probs_rest, own, other, weight_row = refs[groups + 5 + others : groups + 10 + others]
    sums, peak, inverse, scale, mass, tall, tail = refs[-7:]
    h, width = own.shape
    rows = moved_rest.shape[0]
    block = probs.shape[2]

    best = gathered[0][0:1, 0:rows]
    for g in gathered[1:]:
        best = jnp.maximum(best, g[0:1, 0:rows])
    whole = jnp.zeros((1, rows), F32)
    for g in gathered:
        whole += g[1:2, 0:rows] * jnp.exp(g[0:1, 0:rows] - best)
    over = 1.0 / whole
    for j in range(GROUP):
        peak[:, j * rows : (j + 1) * rows] = jnp.broadcast_to(best, (8, rows))
        inverse[:, j * rows : (j + 1) * rows] = jnp.broadcast_to(over, (8, rows))
    for i in range(STEPS):
        scale[i] = jnp.exp(tops[i] - peak[...]) * inverse[...]

    last = weights_rest[...] * (jnp.exp(tops[STEPS, 0:1, 0:rows] - best) * over)
    last_low = last.astype(BF16)
    probs_rest[...] = last_low
    mass[...] = jnp.zeros(mass.shape, F32)
    mass[:, 0:1] = jnp.sum(last, axis=1, keepdims=True)

    def normalise(i):
        part = mass[...]
        for q in range(0, block, 128):
            prob = weights[i, :, q : q + 128] * scale[i, 0:1, q : q + 128]
            probs[i, :, q : q + 128] = prob.astype(BF16)
            part += prob
        mass[...] = part

    accumulate(sums, probs, probs_rest, moved, moved_rest, rest_at, normalise)
    split_pair(sums, own, other)
    row = column_to_row(jnp.sum(mass[...], axis=1, keepdims=True), length, tall)
    weight_row[...] = jnp.broadcast_to(row, weight_row.shape)
    other[h : h + TAIL, :] = tail_block(row, width, tail)


def sums_body(probs, probs_rest, moved, moved_rest, *refs, others, rest_at):
    own, other = refs[others : others + 2]
    sums = refs[-1]
    accumulate(sums, probs, probs_rest, moved, moved_rest, rest_at)
    split_pair(sums, own, other)


def first_pair_body(own, received, weight_row, message, chip_row, tail):
    h, width = own.shape
    message[0:h, :] = (own[...] + received[0:h, :].astype(F32)).astype(BF16)
    length = weight_row.shape[1]
    row = weight_row[0:1, :] + row_of_tail(received[h : h + TAIL, :].astype(F32), width, length)
    chip_row[...] = jnp.broadcast_to(row, chip_row.shape)
    message[h : h + TAIL, :] = tail_block(row, width, tail)


def pair_body(own, received, chip_row, *refs):
    arrived = refs[:-2]
    message, tail = refs[-2:]
    h, width = own.shape
    length = chip_row.shape[1]
    x = own[...] + received[...].astype(F32)
    row = chip_row[0:1, :]
    for m in arrived:
        x += m[0:h, :].astype(F32)
        row += row_of_tail(m[h : h + TAIL, :].astype(F32), width, length)
    message[0:h, :] = x.astype(BF16)
    message[h : h + TAIL, :] = tail_block(row, width, tail)


def finish_body(*refs, count):
    messages = refs[:count]
    own, received, chip_row, class_sums, class_weight = refs[count:]
    h, width = own.shape
    rotations, classes = class_weight.shape[1], class_weight.shape[0]
    length = chip_row.shape[1]
    x = own[...] + received[...].astype(F32)
    row = chip_row[0:1, :]
    for m in messages:
        x += m[0:h, :].astype(F32)
        row += row_of_tail(m[h : h + TAIL, :].astype(F32), width, length)
    class_sums[...] = x
    shape = (classes, length)
    at = lax.broadcasted_iota(jnp.int32, shape, 1)
    mine = at - at // classes * classes == lax.broadcasted_iota(jnp.int32, shape, 0)
    pick = lax.broadcasted_iota(jnp.int32, (length, rotations), 0) // classes
    pick = pick == lax.broadcasted_iota(jnp.int32, (length, rotations), 1)
    pick = pick.astype(F32).astype(BF16)
    high, mid, low = [
        contract(
            jnp.where(mine, jnp.broadcast_to(part, shape), 0.0).astype(BF16), pick, ((1,), (0,))
        )
        for part in spread(row)
    ]
    class_weight[...] = (low + mid) + high


VMEM = pl.BlockSpec(memory_space=pltpu.VMEM)


def make_on_device(dom, cls):
    pairs = dom // 2

    def swap(x, axis, size, k):
        return lax.ppermute(x, axis, [(i, i ^ k) for i in range(size)])

    def on_device(particles, references, noise_weight):
        rows, part_width = particles.shape
        classes, rotations, width = references.shape
        h = classes * rotations
        length = -(-h // width) * width
        block = GROUP * rows
        shape = jax.ShapeDtypeStruct

        def call(body, shapes, name, scratch=(), limit=2, aliases=None, inputs=VMEM, flops=1):
            def run(*args):
                specs = [inputs] * len(args)
                spec = pltpu.PrefetchScalarGridSpec(
                    num_scalar_prefetch=0,
                    grid=(),
                    in_specs=specs,
                    out_specs=[VMEM] * len(shapes),
                    scratch_shapes=list(scratch),
                )
                params = pltpu.CompilerParams(vmem_limit_bytes=limit * 1024 * 1024)
                return pl.pallas_call(
                    body,
                    grid_spec=spec,
                    out_shape=shapes,
                    compiler_params=params,
                    input_output_aliases=aliases or {},
                    cost_estimate=pl.CostEstimate(flops=flops, transcendentals=0, bytes_accessed=1),
                    name=name,
                )(*args)

            return run

        pieces = [particles] + [swap(particles, "cls", cls, k) for k in range(1, cls)]

        tables = phase_tables()
        ref_rows = references.transpose(1, 0, 2).reshape(h, width)
        message, *angles, pieces[0] = call(
            lambda *r: begin_body(*r, width=width),
            [shape((h + TAIL, width), BF16)]
            + [shape(tables.shape[1:], F32)] * 2
            + [shape(particles.shape, BF16)],
            "begin",
            [
                pltpu.VMEM((h, width), F32),
                pltpu.VMEM((1, HALF), F32),
                pltpu.VMEM(tables.shape, F32),
                pltpu.VMEM((length, 128), F32),
                pltpu.VMEM((TAIL, width), F32),
                pltpu.SemaphoreType.DMA((4,)),
            ],
            inputs=pl.BlockSpec(memory_space=pltpu.HBM),
        )(
            *[
                pltpu.with_memory_space_constraint(x, pltpu.HBM)
                for x in (ref_rows, noise_weight.reshape(1, HALF), jnp.asarray(tables), particles)
            ],
        )

        even = [message] + [None] * (pairs - 1)
        for k in range(1, pairs):
            if not k & (k - 1):
                even[k] = swap(message, "dom", dom, 2 * k)
        odd = [swap(message, "dom", dom, 1)]

        *moved, moved_rest = call(
            lambda *r: shift_body(*r, parts=cls, pairs=pairs, width=width),
            [pltpu.VMEM((MAIN * rows, 2 * width), BF16)] * pairs + [shape((rows, F), BF16)],
            "shift",
            flops=10**10,
            limit=2,
            scratch=[pltpu.VMEM((rows, F), F32)] * 2,
        )(*pieces, *angles)

        for k in range(1, pairs):
            if k & (k - 1):
                source = k & (k - 1)
                moved_rest, even[source] = lax.optimization_barrier((moved_rest, even[source]))
                even[k] = swap(even[source], "dom", dom, 2 * (k & -k))

        held = pltpu.VMEM((MAIN * rows, 2 * width), BF16)
        partial = []
        stages = [[0]] + [list(range(1 << t, 2 << t)) for t in range((pairs - 1).bit_length())]
        for n, stage in enumerate(stages):
            last = stage[-1] == pairs - 1
            count = len(stage)
            rest = [k for k in range(pairs) if k not in stage]
            first_held = 4 if last else 3
            after = 3 * count + 1 + len(partial)
            aliases = {2 * count + m: first_held + k for m, k in enumerate(stage)}
            aliases |= {after + m: first_held + k for m, k in enumerate(rest)}
            if partial:
                aliases |= {3 * count + 1: 0, 3 * count + 2: 1}
            body = last_stage_body if last else stage_body
            options = {} if last else {"first": not partial}
            outs = [pltpu.VMEM((STEPS, h, block), F32), shape((h, rows), F32)]
            scratch = [pltpu.VMEM((h, 2 * width * count), BF16)]
            if last:
                outs += [shape((STEPS + 1, 8, block), F32), shape((8, 128), F32)]
                scratch += [
                    pltpu.VMEM((h, 128), F32),
                    pltpu.VMEM((h, block), F32),
                    pltpu.VMEM((h, block), F32),
                    pltpu.VMEM((STEPS, 8, block), F32),
                ]
            else:
                outs += [shape((8, length), F32)]
                for k in sorted(stages[n + 1] if n == 0 else [j for j in stages[n + 1] if not j & (j - 1)]):
                    if partial:
                        partial[2], even[k] = lax.optimization_barrier((partial[2], even[k]))
                    else:
                        moved_rest, even[k] = lax.optimization_barrier((moved_rest, even[k]))
                    odd.append(swap(even[k], "dom", dom, 1))
            if n > 1:
                for k in stage:
                    if k & (k - 1):
                        partial[2], even[k] = lax.optimization_barrier((partial[2], even[k]))
                        odd.append(swap(even[k], "dom", dom, 1))
            results = call(
                lambda *r: body(
                    *r,
                    count=count,
                    others=len(rest),
                    length=length,
                    rest_at=2 * stage[0] * width,
                    **options,
                ),
                outs + [held] * pairs,
                "score",
                scratch,
                limit=6 if last else 6,
                aliases=aliases,
            )(
                *[m for k in stage for m in (even[k], odd[k])],
                *[moved[k] for k in stage],
                moved_rest,
                *partial,
                *[moved[k] for k in rest],
            )
            partial, moved = list(results[:first_held]), results[first_held:]
        weights, weights_rest, tops, stats = partial

        gathered = [stats] + [swap(stats, "cls", cls, k) for k in range(1, cls)]

        accumulator = pltpu.VMEM((h, 2 * width), F32)
        order = sorted(range(1, pairs), key=lambda k: (k & -k, -k)) + [0]
        sent = {}

        def children(k):
            low = k & -k or pairs
            return [sent[k | 1 << t] for t in range(low.bit_length() - 1)]

        probs, probs_rest, own, other, weight_row, *kept = call(
            lambda *r: first_sums_body(
                *r, groups=cls, others=pairs - 1, length=length, rest_at=order[0] * 2 * width
            ),
            [
                shape((STEPS, h, block), BF16),
                shape((h, rows), BF16),
                shape((h, width), F32),
                shape((h + TAIL, width), BF16),
                shape((8, length), F32),
            ]
            + [held] * (pairs - 1),
            "sums_first",
            aliases={cls + 5 + k: 5 + k for k in range(pairs - 1)},
            limit=2,
            scratch=[
                accumulator,
                pltpu.VMEM((8, block), F32),
                pltpu.VMEM((8, block), F32),
                pltpu.VMEM(tops.shape, F32),
                pltpu.VMEM((h, 128), F32),
                pltpu.VMEM((length, 128), F32),
                pltpu.VMEM((TAIL, width), F32),
            ],
        )(
            *gathered,
            weights,
            weights_rest,
            tops,
            moved[order[0]],
            moved_rest,
            *[moved[k] for k in order[1:]],
        )
        received = swap(other, "dom", dom, 1)
        first, chip_row = call(
            first_pair_body,
            [shape((h + TAIL, width), BF16), shape((8, length), F32)],
            "pair_first",
            [pltpu.VMEM((TAIL, width), F32)],
        )(own, received, weight_row)
        sent[order[0]] = swap(first, "dom", dom, 2 * (order[0] & -order[0]))
        ready = first

        for n, k in enumerate(order[1:]):
            if n:
                probs_rest, ready = lax.optimization_barrier((probs_rest, ready))
            others = pairs - 2 - n
            own, other, *kept = call(
                lambda *r: sums_body(*r, others=others, rest_at=k * 2 * width),
                [shape((h, width), F32), shape((h, width), BF16)] + [held] * others,
                "sums",
                [accumulator],
                aliases={4 + j: 2 + j for j in range(others)},
            )(probs, probs_rest, kept[0], moved_rest, *kept[1:])
            received = swap(other, "dom", dom, 1)
            if k:
                (ready,) = call(
                    pair_body,
                    [shape((h + TAIL, width), BF16)],
                    "pair",
                    [pltpu.VMEM((TAIL, width), F32)],
                )(own, received, chip_row, *children(k))
                sent[k] = swap(ready, "dom", dom, 2 * (k & -k))

        arrived = children(0)
        sums, class_weight = call(
            lambda *r: finish_body(*r, count=len(arrived)),
            [shape((h, width), F32), shape((classes, rotations), F32)],
            "finish",
        )(*arrived, own, received, chip_row)
        return sums.reshape(rotations, classes, width).transpose(1, 0, 2), class_weight

    return on_device


def solution(mesh):
    return jax.shard_map(
        make_on_device(mesh.shape["dom"], mesh.shape["cls"]),
        mesh=mesh,
        in_specs=(P("dom", "cls"), P("cls", None, "dom"), P()),
        out_specs=(P("cls", None, "dom"), P("cls", None)),
        check_vma=False,
    )
```
